32 devices in a mesh: cam: 4 (over y, core), tile: 8 (over z, x).
Axes of the slice: x: 2, y: 2, z: 4, core: 2. Of those that a mesh axis runs over, the one named last changes fastest.
Arguments:
- tokens: bfloat16 [5632, 1024], P(('cam', 'tile')), may hold values from -16 to 16
- ln_gain: float32 [1024], replicated, may hold values from 0.25 to 1.75
- gate_weight: bfloat16 [1024, 2730], P(('cam', 'tile')), may hold values from -0.1875 to 0.1875
- up_weight: bfloat16 [1024, 2730], P(('cam', 'tile')), may hold values from -0.1875 to 0.1875
- down_weight: bfloat16 [2730, 1024], P(None, ('cam', 'tile')), may hold values from -0.109375 to 0.109375
- head_gain: float32 [1024], replicated, may hold values from 0.25 to 1.75
- depth_weight: bfloat16 [1024, 64], replicated, may hold values from -24 to 24
- context_weight: bfloat16 [1024, 128], replicated, may hold values from -3 to 3
- slot_point: int32 [32, 8, 2503], P(('cam', 'tile')), may hold values from 0 to 11263, as said below
- slot_cell: int32 [32, 8, 2503], P(('cam', 'tile')), may hold values from 0 to 2047, as said below
- slot_count: int32 [32, 8], P(('cam', 'tile')), may hold values from 312 to 2503
- conv1_weight: bfloat16 [3, 3, 128, 128], replicated, may hold values from -0.1875 to 0.1875
- conv1_bias: float32 [128], replicated, may hold values from -1.5 to 1.5
- conv2_weight: bfloat16 [3, 3, 128, 128], replicated, may hold values from -0.1875 to 0.1875
- conv2_bias: float32 [128], replicated, may hold values from -1.5 to 1.5
Outputs:
- bev_out: bfloat16 [8, 32, 256, 128], P('cam', 'tile')
The draws below stay inside these ranges and needn't reach their ends.
Inputs may be any that keep to these rules, and one draw needn't show every extreme that they name: slot_point[s, d, k] is a point of source s; the live slots (k < slot_count[s, d]) of one source name distinct points. slot_cell[s, d, k] is a cell of tile d, numbered as in the reference program.
All inputs are finite; a program needn't handle non-finite values.
Results may differ from the reference program's by a relative error of at most 0.013.
The reference program's roundings to bfloat16 on the way count: a program that leaves them out, or rounds other values in their place, can miss the bound.
Values may be sent and summed in bfloat16 or wider, within the bound.
A program may use at most 64 MiB of HBM per device.

```python
import math
import jax
import jax.numpy as jnp
from jax import lax

D = 1024
FF = 2730
BINS = 64
CH = 128
TOK_DEV = 176
ROWS_DEV = 4
GRID_W = 256
SCN = 2
SOURCES = 32
TOKENS = 5632
SCENES = 8
GRID_H = 32
SLOT = 2503
N_CAM = 4
N_TILE = 8


def plan_slots(key):
    sources = N_CAM * N_TILE
    point_total = TOK_DEV * BINS
    busiest = jax.random.randint(jax.random.fold_in(key, 11), (N_CAM,), 0, N_TILE)
    busiest_src = jnp.repeat(busiest, N_TILE)
    loads = jax.random.randint(jax.random.fold_in(key, 12), (sources, N_TILE), SLOT // 8, SLOT // 2 + 1)
    tile_ids = jnp.arange(N_TILE, dtype=jnp.int32)
    counts = jnp.where(tile_ids[None, :] == busiest_src[:, None], SLOT, loads).astype(jnp.int32)
    offsets = jnp.cumsum(counts, axis=1) - counts
    source_keys = jax.random.split(jax.random.fold_in(key, 13), sources)
    orders = jax.vmap(lambda single: jax.random.permutation(single, point_total))(source_keys)
    places = (offsets[:, :, None] + jnp.arange(SLOT, dtype=jnp.int32)[None, None, :]) % point_total
    points = jnp.take_along_axis(orders, places.reshape(sources, -1), axis=1)
    return (counts, points.reshape(sources, N_TILE, SLOT).astype(jnp.int32))


def draw_slot_point(key, part):
    counts, points = plan_slots(key)
    return points


def draw_slot_count(key, part):
    counts, points = plan_slots(key)
    return counts


def draw_slot_cell(key, part):
    return jax.random.randint(jax.random.fold_in(key, 21), (N_CAM * N_TILE, N_TILE, SLOT), 0, SCN * ROWS_DEV * GRID_W).astype(jnp.int32)


def draw_tokens(key, part):
    row_scale = jnp.exp(jax.random.uniform(jax.random.fold_in(key, 31), (TOKENS, 1), jnp.float32, math.log(0.3), math.log(3.0)))
    col_scale = jnp.exp(jax.random.uniform(jax.random.fold_in(key, 32), (1, D), jnp.float32, math.log(0.3), math.log(3.0)))
    noise = jax.random.normal(jax.random.fold_in(key, 33), (TOKENS, D), jnp.float32)
    values = row_scale * col_scale * noise
    return jnp.clip(values, -16.0, 16.0).astype(jnp.bfloat16)


def draw_depth_weight(key, part):
    base = jax.random.normal(jax.random.fold_in(key, 41), (D, BINS), jnp.float32) / math.sqrt(D)
    return jnp.clip(base, -24.0, 24.0).astype(jnp.bfloat16)


def steps_of(key, shape, cuts, smallest, top_value):
    factor_of, own = 1.0, jax.random.fold_in(key, 6)
    for position, shards_of in cuts:
        draws = jnp.exp(jax.random.uniform(jax.random.fold_in(own, position), (shards_of,), jnp.float32, smallest / len(cuts), top_value / len(cuts)))
        factor_of = factor_of * jnp.repeat(draws, shape[position] // shards_of).reshape([-1 if axis == position else 1 for axis in range(len(shape))])
    return factor_of


def normal_values(rng, shape, width, most, shards=(), kind=jnp.bfloat16):
    level = steps_of(rng, shape, shards, -0.22, 0.18) if shards else 1.0
    drawn = jax.random.normal(rng, shape, jnp.float32) * width * level
    return jnp.minimum(jnp.maximum(drawn, -most), most).astype(kind)


def setup_inputs(seed: int = 0) -> dict:
    streams_of = jax.random.split(jax.random.key(seed), 16)
    tokens = draw_tokens(jax.random.fold_in(streams_of[15], 71), 0)
    ln_gain = jnp.clip(1.0 + 0.15 * jax.random.normal(streams_of[1], (D,), jnp.float32), 0.25, 1.75)
    gate_weight = normal_values(streams_of[2], (D, FF), D ** -0.5, 0.1875, ((0, 32),))
    up_weight = normal_values(streams_of[3], (D, FF), D ** -0.5, 0.1875, ((0, 32),))
    down_weight = normal_values(streams_of[4], (FF, D), FF ** -0.5, 0.109375, ((1, 32),))
    head_gain = jnp.clip(1.0 + 0.15 * jax.random.normal(streams_of[5], (D,), jnp.float32), 0.25, 1.75)
    depth_weight = draw_depth_weight(jax.random.fold_in(streams_of[15], 71), 0)
    context_weight = normal_values(streams_of[7], (D, CH), (D // 256) ** -0.5, 3.0)
    slot_point = draw_slot_point(jax.random.fold_in(streams_of[15], 71), 0)
    slot_cell = draw_slot_cell(jax.random.fold_in(streams_of[15], 71), 0)
    slot_count = draw_slot_count(jax.random.fold_in(streams_of[15], 71), 0)
    conv1_weight = normal_values(streams_of[11], (3, 3, CH, CH), (9 * CH) ** -0.5, 0.1875)
    conv1_bias = normal_values(streams_of[12], (CH,), 0.3, 1.5, (), jnp.float32)
    conv2_weight = normal_values(streams_of[13], (3, 3, CH, CH), (9 * CH) ** -0.5, 0.1875)
    conv2_bias = normal_values(streams_of[14], (CH,), 0.3, 1.5, (), jnp.float32)
    return {"tokens": tokens, "ln_gain": ln_gain, "gate_weight": gate_weight, "up_weight": up_weight, "down_weight": down_weight, "head_gain": head_gain, "depth_weight": depth_weight, "context_weight": context_weight, "slot_point": slot_point, "slot_cell": slot_cell, "slot_count": slot_count, "conv1_weight": conv1_weight, "conv1_bias": conv1_bias, "conv2_weight": conv2_weight, "conv2_bias": conv2_bias}


def layer_norm(values, gain):
    center = values - lax.optimization_barrier(jnp.mean(values, axis=-1, keepdims=True))
    spread = lax.optimization_barrier(jnp.mean(center * center, axis=-1, keepdims=True))
    return center * lax.rsqrt(spread + 1e-06) * gain

def conv_rows(extended, weight):
    scenes = extended.shape[0]
    out_rows = extended.shape[1] - 2
    columns = extended.shape[2]
    padded = jnp.pad(extended, ((0, 0), (0, 0), (1, 1), (0, 0)))
    total = jnp.zeros((scenes * out_rows * columns, weight.shape[3]), jnp.float32)
    for row_shift in range(3):
        for col_shift in range(3):
            window = padded[:, row_shift:row_shift + out_rows, col_shift:col_shift + columns, :]
            window = window.reshape(-1, weight.shape[2])
            total = total + jnp.dot(window, weight[row_shift, col_shift], preferred_element_type=jnp.float32)
    return total.reshape(scenes, out_rows, columns, weight.shape[3])

def lift_source(token_rows, ln_gain, gate_weight, up_weight, down_weight, head_gain, depth_weight, context_weight, points, counts):
    inputs = token_rows.astype(jnp.float32)
    normed = layer_norm(inputs, ln_gain).astype(jnp.bfloat16)
    gate_full = jnp.dot(normed, gate_weight, preferred_element_type=jnp.float32)
    up_full = jnp.dot(normed, up_weight, preferred_element_type=jnp.float32)
    hidden = (jax.nn.silu(gate_full) * up_full).astype(jnp.bfloat16)
    updated = inputs + jnp.dot(hidden, down_weight, preferred_element_type=jnp.float32)
    head_input = layer_norm(updated, head_gain).astype(jnp.bfloat16)
    logits = jnp.dot(head_input, depth_weight, preferred_element_type=jnp.float32)
    context = jnp.dot(head_input, context_weight, preferred_element_type=jnp.float32).astype(jnp.bfloat16)
    context = lax.optimization_barrier(context).astype(jnp.float32)
    depth = jax.nn.softmax(logits, axis=-1)
    point_ids = points.reshape(-1)
    live = (jnp.arange(SLOT, dtype=jnp.int32)[None, :] < counts[:, None]).reshape(-1)
    weight_live = jnp.where(live, depth.reshape(-1)[point_ids], 0.0)
    lifted = weight_live[:, None] * context[point_ids // BINS]
    return lifted

def scene_block(grid):
    scene = grid[None]
    extended = jnp.pad(scene, ((0, 0), (1, 1), (0, 0), (0, 0)))
    return (scene, extended)

def reference(tokens, ln_gain, gate_weight, up_weight, down_weight, head_gain, depth_weight, context_weight, slot_point, slot_cell, slot_count, conv1_weight, conv1_bias, conv2_weight, conv2_bias):
    cell_count = SCN * ROWS_DEV * GRID_W

    def one_source(source, accum):
        token_rows = lax.dynamic_slice_in_dim(tokens, source * TOK_DEV, TOK_DEV, 0)
        lifted = lift_source(token_rows, ln_gain, gate_weight, up_weight, down_weight, head_gain, depth_weight, context_weight, slot_point[source], slot_count[source])
        group = source // N_TILE
        flat_cells = (jnp.arange(N_TILE, dtype=jnp.int32)[:, None] * cell_count + slot_cell[source]).reshape(-1)
        return accum.at[group, flat_cells].add(lifted)
    accum = lax.fori_loop(0, SOURCES, one_source, jnp.zeros((N_CAM, N_TILE * cell_count, CH), jnp.float32))
    bev = accum.astype(jnp.bfloat16).reshape(N_CAM, N_TILE, SCN, ROWS_DEV, GRID_W, CH)
    bev = bev.transpose(0, 2, 1, 3, 4, 5).reshape(SCENES, GRID_H, GRID_W, CH)

    def convolve(grid):
        scene, extended = scene_block(grid)
        middle = jnp.maximum(conv_rows(extended, conv1_weight) + conv1_bias, 0.0).astype(jnp.bfloat16)
        middle_ext = jnp.pad(middle, ((0, 0), (1, 1), (0, 0), (0, 0)))
        result = scene.astype(jnp.float32) + conv_rows(middle_ext, conv2_weight) + conv2_bias
        return result.astype(jnp.bfloat16)[0]
    return lax.map(convolve, bev)
```

```python
import functools

import jax
import jax.numpy as jnp
from jax import lax
from jax.experimental import pallas as pl
from jax.experimental.pallas import tpu as pltpu
from jax.sharding import PartitionSpec as P

ROWS_DEV = 4
GRID_W = 256
SCN = 2
CHUNK = 512
LANES = 128
MESH = pl.DeviceIdType.MESH


def layer_norm(values, gain):
    center = values - jnp.mean(values, axis=-1, keepdims=True)
    spread = jnp.mean(center * center, axis=-1, keepdims=True)
    return center * lax.rsqrt(spread + 1e-06) * gain


def remote(src, dst, send, recv, cam, tile):
    return pltpu.make_async_remote_copy(
        src_ref=src,
        dst_ref=dst,
        send_sem=send,
        recv_sem=recv,
        device_id={"cam": cam, "tile": tile},
        device_id_type=MESH,
    )


def soft_table(scores, bins):
    logits = scores[:bins]
    top = jnp.max(logits, axis=0, keepdims=True)
    raised = jnp.exp(logits - top)
    depth = raised / jnp.sum(raised, axis=0, keepdims=True)
    return jnp.concatenate([depth, scores[bins:]], axis=0).astype(jnp.bfloat16)


class Exchange:
    def __init__(self, tiles, own, whole, recv, up, down, side, core, pair):
        self.cam, self.tile = lax.axis_index("cam"), lax.axis_index("tile")
        self.tiles, self.depth = tiles, tiles // 2
        self.y, self.c = self.cam // 2, lax.rem(self.cam, 2)
        self.z, self.x = self.tile // 2, lax.rem(self.tile, 2)
        self.own, self.whole, self.recv = own, whole, recv
        self.up, self.down, self.side, self.core, self.pair = up, down, side, core, pair
        self.rows = own.shape[2]
        self.span = ((0, 2), (2, 1))

    def shard(self, y, c, z, x):
        return (2 * y + c) * self.tiles + 2 * z + x

    def block(self, kind, shard):
        first, count = self.span[kind]
        rows = pl.ds(pl.multiple_of(shard * self.rows, self.rows), self.rows)
        return self.whole.at[pl.ds(first, count), rows, :]

    def mine(self, kind, half):
        first, count = self.span[kind]
        return self.own.at[half, pl.ds(first, count)]

    def to(self, route, kind, y, z, x):
        shard = self.shard(y, self.c, z, x)
        block = self.block(kind, shard)
        q = 2 * z + x
        got = self.recv.at[kind, shard]
        if route == "up":
            return remote(block, block, self.up.at[kind, q], got, self.cam, self.tile + 2)
        if route == "down":
            return remote(block, block, self.down.at[kind, q], got, self.cam, self.tile - 2)
        if route == "side":
            other = 2 * (1 - self.y) + self.c
            return remote(block, block, self.side.at[kind, q], got, other, self.tile)
        other = 2 * self.y + 1 - self.c
        return remote(block, block, self.core.at[kind, y, q], got, other, self.tile)

    def across(self, kind):
        shard = self.shard(self.y, self.c, self.z, self.x)
        return remote(
            self.mine(kind, 1 - self.x),
            self.block(kind, shard),
            self.pair.at[kind],
            self.recv.at[kind, shard],
            self.cam,
            self.tile + 1 - 2 * self.x,
        )

    def wait(self, kind, y, c, z, x):
        shard = self.shard(y, c, z, x)
        block = self.block(kind, shard)
        remote(
            block, block, self.pair.at[kind], self.recv.at[kind, shard], self.cam, self.tile
        ).wait_recv()

    def spread(self, kind, x):
        def go_up():
            self.to("up", kind, self.y, self.z, x).start()

        def go_down():
            self.to("down", kind, self.y, self.z, x).start()

        pl.when(self.z + 1 < self.depth)(go_up)
        pl.when(self.z > 0)(go_down)
        self.to("side", kind, self.y, self.z, x).start()
        self.to("core", kind, self.y, self.z, x).start()

    def relay(self, kind, d):
        for step in range(2):
            x = self.x if step == 0 else 1 - self.x

            def below():
                z = self.z - d
                self.wait(kind, self.y, self.c, z, x)

                def go_up():
                    self.to("up", kind, self.y, z, x).start()

                pl.when(self.z + 1 < self.depth)(go_up)
                self.to("side", kind, self.y, z, x).start()
                self.to("core", kind, self.y, z, x).start()

            def above():
                z = self.z + d
                self.wait(kind, self.y, self.c, z, x)

                def go_down():
                    self.to("down", kind, self.y, z, x).start()

                pl.when(self.z > 0)(go_down)
                self.to("side", kind, self.y, z, x).start()
                self.to("core", kind, self.y, z, x).start()

            pl.when(self.z - d >= 0)(below)
            pl.when(self.z + d < self.depth)(above)

    def crossed(self, kind, d):
        y = 1 - self.y

        def take(z):
            for step in range(2):
                x = self.x if step == 0 else 1 - self.x
                self.wait(kind, y, self.c, z, x)
                self.to("core", kind, y, z, x).start()

        if d == 0:
            take(self.z)
            return
        pl.when(self.z - d >= 0)(lambda: take(self.z - d))
        pl.when(self.z + d < self.depth)(lambda: take(self.z + d))

    def beside(self, kind, y):
        for z in range(self.depth):
            for x in range(2):
                self.wait(kind, y, 1 - self.c, z, x)

    def finish(self):
        for kind in range(2):
            self.across(kind).wait_send()
            for q in range(self.tiles):
                z, x = q // 2, q % 2

                def up():
                    self.to("up", kind, self.y, z, x).wait_send()

                def down():
                    self.to("down", kind, self.y, z, x).wait_send()

                pl.when((self.z >= z) & (self.z + 1 < self.depth))(up)
                pl.when((self.z <= z) & (self.z > 0))(down)
                self.to("side", kind, self.y, z, x).wait_send()
                for y in range(2):
                    self.to("core", kind, y, z, x).wait_send()


def feed_forward(ex, tokens, gain, guest, normed, gate, up, hidden, kept, sent, came, sems):
    local, tok_send, tok_recv, part_send, part_recv = sems
    count = tokens.shape[0]
    mate = ex.tile + 1 - 2 * ex.x
    token_copy = remote(tokens, guest, tok_send, tok_recv, ex.cam, mate)
    me = ex.shard(ex.y, ex.c, ex.z, ex.x)
    copies = [
        pltpu.make_async_copy(ex.mine(kind, ex.x), ex.block(kind, me), local.at[kind])
        for kind in range(2)
    ]
    ex.across(0).start()
    for copy in copies:
        copy.start()
    copies[0].wait()
    ex.spread(0, ex.x)
    token_copy.start()
    ex.across(1).start()
    normed[:count] = layer_norm(tokens[...].astype(jnp.float32), gain[...]).astype(jnp.bfloat16)
    ex.wait(0, ex.y, ex.c, ex.z, 1 - ex.x)
    ex.spread(0, 1 - ex.x)
    ex.relay(0, 1)
    copies[1].wait()
    token_copy.wait_recv()
    normed[count:] = layer_norm(guest[...].astype(jnp.float32), gain[...]).astype(jnp.bfloat16)
    ex.crossed(0, 0)
    for d in range(2, ex.depth):
        ex.relay(0, d)
        ex.crossed(0, d - 1)
    ex.spread(1, ex.x)
    ex.wait(1, ex.y, ex.c, ex.z, 1 - ex.x)
    ex.spread(1, 1 - ex.x)
    wide = ex.rows * ex.tiles

    def project(cam, first):
        rows = pl.ds(pl.multiple_of(cam * wide, wide), wide)
        for which, total in ((0, gate), (1, up)):
            got = jnp.dot(
                normed[:, rows], ex.whole[which, rows, :], preferred_element_type=jnp.float32
            )
            if first:
                total[...] = got
            else:
                total[...] += got

    def columns(piece):
        rows = pl.ds(pl.multiple_of(piece * LANES, LANES), LANES)
        got = lax.dot_general(
            hidden[...],
            ex.whole[2, rows, :],
            (((1,), (1,)), ((), ())),
            preferred_element_type=jnp.float32,
        )
        kept[piece] = got[:count]
        sent[piece] = got[count:]
        part(piece).start()

    def part(piece):
        return remote(
            sent.at[piece], came.at[piece], part_send.at[piece], part_recv.at[piece], ex.cam, mate
        )

    project(2 * ex.y + ex.c, True)
    ex.relay(1, 1)
    ex.beside(0, ex.y)
    project(2 * ex.y + 1 - ex.c, False)
    ex.crossed(0, ex.depth - 1)
    for d in range(2, ex.depth):
        ex.relay(1, d)
    project(2 * (1 - ex.y) + ex.c, False)
    ex.beside(0, 1 - ex.y)
    project(2 * (1 - ex.y) + 1 - ex.c, False)
    value = gate[...]
    hidden[...] = (value / (1.0 + jnp.exp(-value)) * up[...]).astype(jnp.bfloat16)
    pieces = wide // LANES
    for half in range(pieces):
        columns((2 * ex.y + ex.c) * pieces + half)
    for d in range(ex.depth):
        ex.crossed(1, d)
    ex.beside(1, ex.y)
    for half in range(pieces):
        columns((2 * ex.y + 1 - ex.c) * pieces + half)
    for half in range(pieces):
        columns((2 * (1 - ex.y) + ex.c) * pieces + half)
    ex.beside(1, 1 - ex.y)
    for half in range(pieces):
        columns((2 * (1 - ex.y) + 1 - ex.c) * pieces + half)
    for piece in range(kept.shape[0]):
        part(piece).wait_recv()
    blocks = [kept[piece] + came[piece] for piece in range(kept.shape[0])]
    updated = tokens[...].astype(jnp.float32) + jnp.concatenate(blocks, axis=1)

    def finish():
        token_copy.wait_send()
        for piece in range(kept.shape[0]):
            part(piece).wait_send()
        ex.finish()

    return updated, finish


def splat(table, held, slots, total, tiles, me, bins, arrived):
    half, wide = total.shape
    tokens = table.shape[1]
    chunks = slots.shape[2] // CHUNK
    total[...] = jnp.zeros_like(total)
    held[0] = table[...]

    def one_source(k, carry):
        arrived(k)
        source = lax.rem(me + k, tiles)

        def step(i, inner):
            start = pl.multiple_of(i * CHUNK, CHUNK)
            packed = slots[source, :, pl.ds(start, CHUNK)]
            point, cell = packed // 65536, packed % 65536
            token, depth_bin = point // bins, point % bins
            token_ids = lax.broadcasted_iota(jnp.int32, (tokens, CHUNK), 0)
            pick = jnp.where(token_ids == token, 1.0, 0.0).astype(jnp.bfloat16)
            got = jnp.dot(held[k], pick, preferred_element_type=jnp.float32)
            bin_ids = lax.broadcasted_iota(jnp.int32, (bins, CHUNK), 0)
            weight = jnp.sum(
                jnp.where(bin_ids == depth_bin, got[:bins], 0.0), axis=0, keepdims=True
            )
            upper = cell >= half
            low = jnp.where(upper, 0.0, weight) * got[bins:]
            high = jnp.where(upper, weight, 0.0) * got[bins:]
            lifted = jnp.concatenate([low, high], axis=0).astype(jnp.bfloat16)
            local = jnp.where(upper, cell - half, cell)
            cell_ids = lax.broadcasted_iota(jnp.int32, (half, CHUNK), 0)
            place = jnp.where(cell_ids == local, 1.0, 0.0).astype(jnp.bfloat16)
            total[...] += lax.dot_general(
                place, lifted, (((1,), (1,)), ((), ())), preferred_element_type=jnp.float32
            )
            return inner

        return lax.fori_loop(0, chunks, step, carry)

    lax.fori_loop(0, tiles, one_source, 0)


def widen(source, index, wide, row):
    value = source[index].astype(jnp.float32)
    columns, channels = value.shape
    places = lax.broadcasted_iota(jnp.int32, (columns, channels), 0)
    left = jnp.where(places == 0, 0.0, pltpu.roll(value, 1, 0))
    right = jnp.where(places == columns - 1, 0.0, pltpu.roll(value, columns - 1, 0))
    wide[row] = jnp.concatenate([left, value, right], axis=1).astype(jnp.bfloat16)


def convolve(wide, row, weight):
    total = None
    for shift in range(3):
        got = jnp.dot(wide[row + shift], weight[shift], preferred_element_type=jnp.float32)
        total = got if total is None else total + got
    return total


def program(fused, tiles, bins, *refs):
    if fused:
        (tokens, gain, own, head_gain, head, slot_in, w1, b1, w2, b2, out) = refs[:11]
        (slots, table, held, total, ext, wide, mid, wide_mid) = refs[11:19]
        (slot_send, slot_recv, table_send, table_recv, halo_send, halo_recv) = refs[19:25]
        (whole, guest, normed, gate, up, hidden, kept, sent, came) = refs[25:34]
        (recv, zup, zdown, side, core, pair) = refs[34:40]
        sems = refs[40:45]
    else:
        (table_in, slot_in, w1, b1, w2, b2, out) = refs[:7]
        (slots, table, held, total, ext, wide, mid, wide_mid) = refs[7:15]
        (slot_send, slot_recv, table_send, table_recv, halo_send, halo_recv) = refs[15:21]
    cam, me = lax.axis_index("cam"), lax.axis_index("tile")
    barrier = pltpu.get_barrier_semaphore()

    def greet(k, carry):
        other = lax.rem(me + k, tiles)
        pl.semaphore_signal(
            barrier, inc=1, device_id={"cam": cam, "tile": other}, device_id_type=MESH
        )
        return carry

    lax.fori_loop(1, tiles, greet, 0)
    extra = 0
    if fused:
        y, c = cam // 2, lax.rem(cam, 2)
        for other in (2 * (1 - y) + c, 2 * y + 1 - c):
            pl.semaphore_signal(
                barrier, inc=1, device_id={"cam": other, "tile": me}, device_id_type=MESH
            )
            extra += 1
    pl.semaphore_wait(barrier, tiles - 1 + extra)

    def slot_copy(k):
        other = lax.rem(me + k, tiles)
        return remote(slot_in.at[other], slots.at[me], slot_send.at[k], slot_recv.at[k], cam, other)

    def slot_wait(k):
        source = lax.rem(me - k + tiles, tiles)
        remote(
            slot_in.at[me], slots.at[source], slot_send.at[k], slot_recv.at[k], cam, me
        ).wait_recv()

    def slot_start(k, carry):
        slot_copy(k).start()
        return carry

    def slot_finish(k, carry):
        slot_wait(k)
        slot_copy(k).wait_send()
        return carry

    lax.fori_loop(1, tiles, slot_start, 0)
    own_slots = pltpu.make_async_copy(slot_in.at[me], slots.at[me], slot_send.at[0])
    own_slots.start()
    if fused:
        ex = Exchange(tiles, own, whole, recv, zup, zdown, side, core, pair)
        updated, finish = feed_forward(
            ex, tokens, gain, guest, normed, gate, up, hidden, kept, sent, came, sems
        )
        head_input = layer_norm(updated, head_gain[...]).astype(jnp.bfloat16)
        scores = lax.dot_general(
            head[...], head_input, (((1,), (1,)), ((), ())), preferred_element_type=jnp.float32
        )
        table[...] = soft_table(scores, bins)
    else:
        table[...] = table_in[...]

    def table_copy(k):
        other = lax.rem(me - k + tiles, tiles)
        return remote(table, held.at[k], table_send.at[k], table_recv.at[k], cam, other)

    def table_start(k, carry):
        table_copy(k).start()
        return carry

    def table_finish(k, carry):
        table_copy(k).wait_send()
        return carry

    lax.fori_loop(1, tiles, table_start, 0)
    own_slots.wait()
    lax.fori_loop(1, tiles, slot_finish, 0)

    def arrived(k):
        pl.when(k > 0)(lambda: table_copy(k).wait_recv())

    splat(table, held, slots, total, tiles, me, bins, arrived)
    channels = total.shape[1] // 2
    per_scene = ROWS_DEV * GRID_W
    for scene in range(SCN):
        for row in range(ROWS_DEV):
            start = scene * per_scene + row * GRID_W
            side_of, first = divmod(start, total.shape[0])
            ext[scene, 2 + row] = total[
                first : first + GRID_W, side_of * channels : (side_of + 1) * channels
            ].astype(jnp.bfloat16)

    def halo(which):
        if which == 0:
            src, dst, other = ext.at[:, 2:4], ext.at[:, ROWS_DEV + 2 : ROWS_DEV + 4], me - 1
        else:
            src, dst, other = ext.at[:, ROWS_DEV : ROWS_DEV + 2], ext.at[:, 0:2], me + 1
        return remote(src, dst, halo_send.at[which], halo_recv.at[which], cam, other)

    blank = jnp.zeros((SCN, 2, GRID_W, channels), jnp.bfloat16)

    def first_tile():
        ext[:, 0:2] = blank

    def last_tile():
        ext[:, ROWS_DEV + 2 : ROWS_DEV + 4] = blank

    has_before, has_after = me > 0, me + 1 < tiles
    pl.when(has_before)(lambda: halo(0).start())
    pl.when(has_after)(lambda: halo(1).start())
    pl.when(me == 0)(first_tile)
    pl.when(me + 1 == tiles)(last_tile)
    rows_ext = ROWS_DEV + 4
    for scene in range(SCN):
        for row in range(2, ROWS_DEV + 2):
            widen(ext, (scene, row), wide, scene * rows_ext + row)
    pl.when(has_before)(lambda: halo(1).wait_recv())
    pl.when(has_after)(lambda: halo(0).wait_recv())
    for scene in range(SCN):
        for row in (0, 1, ROWS_DEV + 2, ROWS_DEV + 3):
            widen(ext, (scene, row), wide, scene * rows_ext + row)
    rows_mid = ROWS_DEV + 2
    for scene in range(SCN):
        for row in range(rows_mid):
            value = jnp.maximum(convolve(wide, scene * rows_ext + row, w1) + b1[...], 0.0)
            if row == 0:
                value = jnp.where(has_before, value, 0.0)
            if row == rows_mid - 1:
                value = jnp.where(has_after, value, 0.0)
            mid[scene, row] = value.astype(jnp.bfloat16)
            widen(mid, (scene, row), wide_mid, scene * rows_mid + row)
    for scene in range(SCN):
        for row in range(ROWS_DEV):
            value = convolve(wide_mid, scene * rows_mid + row, w2) + b2[...]
            value = ext[scene, 2 + row].astype(jnp.float32) + value
            out[scene, row] = value.astype(jnp.bfloat16)
    pl.when(has_before)(lambda: halo(0).wait_send())
    pl.when(has_after)(lambda: halo(1).wait_send())
    lax.fori_loop(1, tiles, table_finish, 0)
    if fused:
        finish()


def run(fused, arrays, slots, weights, sizes):
    tiles, bins, channels, token_count = sizes
    cells = SCN * ROWS_DEV * GRID_W
    dma = pltpu.SemaphoreType.DMA
    bf16, f32 = jnp.bfloat16, jnp.float32
    scratch = [
        pltpu.VMEM(slots.shape, jnp.int32),
        pltpu.VMEM((bins + channels, token_count), bf16),
        pltpu.VMEM((tiles, bins + channels, token_count), bf16),
        pltpu.VMEM((cells // 2, 2 * channels), f32),
        pltpu.VMEM((SCN, ROWS_DEV + 4, GRID_W, channels), bf16),
        pltpu.VMEM((SCN * (ROWS_DEV + 4), GRID_W, 3 * channels), bf16),
        pltpu.VMEM((SCN, ROWS_DEV + 2, GRID_W, channels), bf16),
        pltpu.VMEM((SCN * (ROWS_DEV + 2), GRID_W, 3 * channels), bf16),
        dma((tiles,)),
        dma((tiles,)),
        dma((tiles,)),
        dma((tiles,)),
        dma((2,)),
        dma((2,)),
    ]
    if fused:
        tokens, own = arrays[0], arrays[2]
        count, width = tokens.shape
        cams = lax.axis_size("cam")
        half = own.shape[3]
        pieces = width // LANES
        scratch += [
            pltpu.VMEM((3, width, half), bf16),
            pltpu.VMEM((count, width), bf16),
            pltpu.VMEM((2 * count, width), bf16),
            pltpu.VMEM((2 * count, half), f32),
            pltpu.VMEM((2 * count, half), f32),
            pltpu.VMEM((2 * count, half), bf16),
            pltpu.VMEM((pieces, count, LANES), f32),
            pltpu.VMEM((pieces, count, LANES), f32),
            pltpu.VMEM((pieces, count, LANES), f32),
            dma((2, cams * tiles)),
            dma((2, tiles)),
            dma((2, tiles)),
            dma((2, tiles)),
            dma((2, 2, tiles)),
            dma((2,)),
            dma((2,)),
            dma,
            dma,
            dma((pieces,)),
            dma((pieces,)),
        ]
    operands = [*arrays, slots, *weights]
    return pl.pallas_call(
        functools.partial(program, fused, tiles, bins),
        out_shape=jax.ShapeDtypeStruct((SCN, ROWS_DEV, GRID_W, channels), bf16),
        in_specs=[pl.BlockSpec(memory_space=pltpu.VMEM)] * len(operands),
        out_specs=pl.BlockSpec(memory_space=pltpu.VMEM),
        scratch_shapes=scratch,
        compiler_params=pltpu.CompilerParams(
            collective_id=0, has_side_effects=True, vmem_limit_bytes=60 * 1024 * 1024
        ),
    )(*operands)


def packed_slots(slot_point, slot_cell, slot_count, points):
    tiles, slots = slot_point.shape[1:]
    live = jnp.arange(slots, dtype=jnp.int32)[None, :] < slot_count.reshape(tiles, 1)
    packed = jnp.where(live, slot_point.reshape(tiles, slots), points) * 65536
    packed = packed + slot_cell.reshape(tiles, slots)
    packed = jnp.pad(packed, ((0, 0), (0, -slots % CHUNK)), constant_values=points * 65536)
    return packed.reshape(tiles, 1, -1)


def table_of(tokens, ln_gain, gate_weight, up_weight, down_weight, head_gain, head):
    inputs = tokens.astype(jnp.float32)
    normed = layer_norm(inputs, ln_gain).astype(jnp.bfloat16)
    axes = ("cam", "tile")
    gate_whole = lax.all_gather(gate_weight, axes, axis=0, tiled=True)
    up_whole = lax.all_gather(up_weight, axes, axis=0, tiled=True)
    gate = jnp.dot(normed, gate_whole, preferred_element_type=jnp.float32)
    up = jnp.dot(normed, up_whole, preferred_element_type=jnp.float32)
    hidden = (jax.nn.silu(gate) * up).astype(jnp.bfloat16)
    down_whole = lax.all_gather(down_weight.T, axes, axis=0, tiled=True)
    contract = (((1,), (1,)), ((), ()))
    branch = lax.dot_general(hidden, down_whole, contract, preferred_element_type=jnp.float32)
    head_input = layer_norm(inputs + branch, head_gain).astype(jnp.bfloat16)
    return lax.dot_general(head, head_input, contract, preferred_element_type=jnp.float32)


def on_device(
    tokens,
    ln_gain,
    gate_weight,
    up_weight,
    down_weight,
    head_gain,
    depth_weight,
    context_weight,
    slot_point,
    slot_cell,
    slot_count,
    conv1_weight,
    conv1_bias,
    conv2_weight,
    conv2_bias,
):
    tiles, cams = lax.axis_size("tile"), lax.axis_size("cam")
    token_count, width = tokens.shape
    bins, channels = depth_weight.shape[1], context_weight.shape[1]
    slots = packed_slots(slot_point, slot_cell, slot_count, token_count * bins)
    weights = [
        conv1_weight.reshape(3, 3 * channels, channels),
        conv1_bias.reshape(1, channels),
        conv2_weight.reshape(3, 3 * channels, channels),
        conv2_bias.reshape(1, channels),
    ]
    head = jnp.concatenate([depth_weight, context_weight], axis=1).T
    sizes = (tiles, bins, channels, token_count)
    rows, units = gate_weight.shape
    fused = cams == 4 and tiles % 2 == 0 and rows % 16 == 0 and (rows * tiles) % LANES == 0
    if not fused:
        scores = table_of(
            tokens, ln_gain, gate_weight, up_weight, down_weight, head_gain, head
        )
        return run(False, [soft_table(scores, bins)], slots, weights, sizes)
    stacked = jnp.stack([gate_weight, up_weight, down_weight.T], axis=0)
    stacked = jnp.pad(stacked, ((0, 0), (0, 0), (0, -units % (2 * LANES))))
    own = stacked.reshape(3, rows, 2, -1).transpose(2, 0, 1, 3)
    arrays = [tokens, ln_gain.reshape(1, width), own, head_gain.reshape(1, width), head]
    return run(True, arrays, slots, weights, sizes)


def solution(mesh):
    return jax.shard_map(
        on_device,
        mesh=mesh,
        in_specs=(
            P(("cam", "tile"), None),
            P(),
            P(("cam", "tile"), None),
            P(("cam", "tile"), None),
            P(None, ("cam", "tile")),
            P(),
            P(),
            P(),
            P(("cam", "tile"), None, None),
            P(("cam", "tile"), None, None),
            P(("cam", "tile"), None),
            P(),
            P(),
            P(),
            P(),
        ),
        out_specs=P("cam", "tile", None, None),
        check_vma=False,
    )
```

```python
import functools

import jax
import jax.numpy as jnp
from jax import lax
from jax.experimental import pallas as pl
from jax.experimental.pallas import tpu as pltpu
from jax.sharding import PartitionSpec as P

ROWS_DEV = 4
GRID_W = 256
SCN = 2
CHUNK = 512
LANES = 128
MESH = pl.DeviceIdType.MESH


def layer_norm(values, gain):
    center = values - jnp.mean(values, axis=-1, keepdims=True)
    spread = jnp.mean(center * center, axis=-1, keepdims=True)
    return center * lax.rsqrt(spread + 1e-06) * gain


def remote(src, dst, send, recv, cam, tile):
    return pltpu.make_async_remote_copy(
        src_ref=src,
        dst_ref=dst,
        send_sem=send,
        recv_sem=recv,
        device_id={"cam": cam, "tile": tile},
        device_id_type=MESH,
    )


def soft_table(scores, bins):
    logits = scores[:bins]
    top = jnp.max(logits, axis=0, keepdims=True)
    raised = jnp.exp(logits - top)
    depth = raised / jnp.sum(raised, axis=0, keepdims=True)
    return jnp.concatenate([depth, scores[bins:]], axis=0).astype(jnp.bfloat16)


class Exchange:
    SPAN = ((0, 1), (1, 1), (2, 1), (0, 2))

    def __init__(self, tiles, own, whole, recv, sends):
        self.cam, self.tile = lax.axis_index("cam"), lax.axis_index("tile")
        self.tiles, self.depth = tiles, tiles // 2
        self.y, self.c = self.cam // 2, lax.rem(self.cam, 2)
        self.z, self.x = self.tile // 2, lax.rem(self.tile, 2)
        self.own, self.whole, self.recv = own, whole, recv
        self.up, self.down, self.side, self.core, self.pair = sends
        self.rows = own.shape[2]

    def shard(self, y, c, z, x):
        return (2 * y + c) * self.tiles + 2 * z + x

    def block(self, kind, shard):
        first, count = self.SPAN[kind]
        rows = pl.ds(pl.multiple_of(shard * self.rows, self.rows), self.rows)
        return self.whole.at[pl.ds(first, count), rows, :]

    def mine(self, kind, half):
        first, count = self.SPAN[kind]
        return self.own.at[half, pl.ds(first, count)]

    def to(self, route, kind, y, z, x):
        shard = self.shard(y, self.c, z, x)
        block = self.block(kind, shard)
        at = (kind, y, 2 * z + x)
        got = self.recv.at[kind, shard]
        if route == "up":
            return remote(block, block, self.up.at[at], got, self.cam, self.tile + 2)
        if route == "down":
            return remote(block, block, self.down.at[at], got, self.cam, self.tile - 2)
        if route == "side":
            other = 2 * (1 - self.y) + self.c
            return remote(block, block, self.side.at[at], got, other, self.tile)
        other = 2 * self.y + 1 - self.c
        return remote(block, block, self.core.at[at], got, other, self.tile)

    def across(self, kind):
        shard = self.shard(self.y, self.c, self.z, self.x)
        return remote(
            self.mine(kind, 1 - self.x),
            self.block(kind, shard),
            self.pair.at[kind],
            self.recv.at[kind, shard],
            self.cam,
            self.tile + 1 - 2 * self.x,
        )

    def wait(self, kind, y, c, z, x):
        shard = self.shard(y, c, z, x)
        block = self.block(kind, shard)
        remote(
            block, block, self.pair.at[kind], self.recv.at[kind, shard], self.cam, self.tile
        ).wait_recv()

    def spread(self, kind, y, x, side):
        def go_up():
            self.to("up", kind, y, self.z, x).start()

        def go_down():
            self.to("down", kind, y, self.z, x).start()

        if side:
            self.to("side", kind, y, self.z, x).start()
        pl.when(self.z + 1 < self.depth)(go_up)
        pl.when(self.z > 0)(go_down)
        self.to("core", kind, y, self.z, x).start()

    def units(self, late):
        mate = 1 - self.x
        if late:
            return ((2, self.y, self.x, True), (2, self.y, mate, True))
        return (
            (0, self.y, self.x, True),
            (1, self.y, self.x, False),
            (1, 1 - self.y, self.x, False),
            (3, self.y, mate, True),
        )

    def relay(self, late, d):
        def take(kind, y, z, x, side, more, route):
            self.wait(kind, y, self.c, z, x)
            if d + 1 < self.depth:
                pl.when(more)(lambda: self.to(route, kind, y, z, x).start())
            if side:
                self.to("side", kind, y, z, x).start()
            self.to("core", kind, y, z, x).start()

        for kind, y, x, side in self.units(late):

            def below():
                take(kind, y, self.z - d, x, side, self.z + 1 < self.depth, "up")

            def above():
                take(kind, y, self.z + d, x, side, self.z > 0, "down")

            pl.when(self.z - d >= 0)(below)
            pl.when(self.z + d < self.depth)(above)

    def crossed(self, late, z):
        for kind, y, x, side in self.units(late):
            if side:
                self.wait(kind, 1 - self.y, self.c, z, x)
                self.to("core", kind, 1 - self.y, z, x).start()

    def crossed_at(self, late, d):
        pl.when(self.z - d >= 0)(lambda: self.crossed(late, self.z - d))
        pl.when(self.z + d < self.depth)(lambda: self.crossed(late, self.z + d))

    def beside(self, late, y, zs):
        for z in zs:
            if late:
                for x in range(2):
                    self.wait(2, y, 1 - self.c, z, x)
            else:
                self.wait(0, y, 1 - self.c, z, self.x)
                self.wait(1, y, 1 - self.c, z, self.x)
                self.wait(3, y, 1 - self.c, z, 1 - self.x)

    def finish(self):
        self.across(3).wait_send()
        self.across(2).wait_send()
        for z in range(self.depth):
            for kind, y, x, side in (*self.units(False), *self.units(True)):

                def up():
                    self.to("up", kind, y, z, x).wait_send()

                def down():
                    self.to("down", kind, y, z, x).wait_send()

                pl.when((self.z >= z) & (self.z + 1 < self.depth))(up)
                pl.when((self.z <= z) & (self.z > 0))(down)
                self.to("core", kind, y, z, x).wait_send()
                if side:
                    self.to("side", kind, y, z, x).wait_send()
                    self.to("core", kind, 1 - y, z, x).wait_send()
        self.to("side", 1, self.y, self.z, self.x).wait_send()


def feed_forward(ex, tokens, gain, guest, normed, gate, up, hidden, kept, sent, came, sems, midway):
    local, tok_send, tok_recv, part_send, part_recv = sems
    count = tokens.shape[0]
    mate = ex.tile + 1 - 2 * ex.x
    token_copy = remote(tokens, guest, tok_send, tok_recv, ex.cam, mate)
    me = ex.shard(ex.y, ex.c, ex.z, ex.x)
    copies = [
        pltpu.make_async_copy(ex.mine(kind, ex.x), ex.block(kind, me), local.at[kind - 2])
        for kind in (3, 2)
    ]
    ex.across(3).start()
    for copy in copies:
        copy.start()
    copies[0].wait()
    ex.to("side", 1, ex.y, ex.z, ex.x).start()
    ex.spread(0, ex.y, ex.x, True)
    ex.spread(1, ex.y, ex.x, False)
    ex.across(2).start()
    token_copy.start()
    ex.wait(1, 1 - ex.y, ex.c, ex.z, ex.x)
    ex.spread(1, 1 - ex.y, ex.x, False)
    ex.wait(3, ex.y, ex.c, ex.z, 1 - ex.x)
    ex.spread(3, ex.y, 1 - ex.x, True)
    ex.relay(False, 1)
    ex.crossed(False, ex.z)
    for d in range(2, ex.depth - 1):
        ex.relay(False, d)
        ex.crossed_at(False, d - 1)
    copies[1].wait()
    ex.spread(2, ex.y, ex.x, True)
    ex.wait(2, ex.y, ex.c, ex.z, 1 - ex.x)
    ex.spread(2, ex.y, 1 - ex.x, True)
    token_copy.wait_recv()
    normed[count:] = layer_norm(guest[...].astype(jnp.float32), gain[...]).astype(jnp.bfloat16)
    wide = ex.rows * ex.tiles
    pieces = wide // LANES
    per_piece = ex.depth // pieces

    def project(cam, first):
        rows = pl.ds(pl.multiple_of(cam * wide, wide), wide)
        for which, total in ((0, gate), (1, up)):
            got = jnp.dot(
                normed[:, rows], ex.whole[which, rows, :], preferred_element_type=jnp.float32
            )
            if first:
                total[...] = got
            else:
                total[...] += got

    def part(piece):
        return remote(
            sent.at[piece], came.at[piece], part_send.at[piece], part_recv.at[piece], ex.cam, mate
        )

    def columns(cam, near):
        piece = cam * pieces + near
        rows = pl.ds(pl.multiple_of(piece * LANES, LANES), LANES)
        got = lax.dot_general(
            hidden[...],
            ex.whole[2, rows, :],
            (((1,), (1,)), ((), ())),
            preferred_element_type=jnp.float32,
        )
        kept[piece] = got[:count]
        sent[piece] = got[count:]
        part(piece).start()

    every = range(ex.depth)
    ex.relay(False, ex.depth - 1)
    midway()
    project(2 * ex.y + ex.c, True)
    ex.crossed_at(False, ex.depth - 2)
    ex.relay(True, 1)
    ex.beside(False, ex.y, every)
    project(2 * ex.y + 1 - ex.c, False)
    ex.crossed_at(False, ex.depth - 1)
    project(2 * (1 - ex.y) + ex.c, False)
    for d in range(2, ex.depth - 1):
        ex.relay(True, d)
    ex.beside(False, 1 - ex.y, every)
    project(2 * (1 - ex.y) + 1 - ex.c, False)
    value = gate[...]
    hidden[...] = (value / (1.0 + jnp.exp(-value)) * up[...]).astype(jnp.bfloat16)
    for turn in range(pieces):
        near = lax.rem(ex.z // per_piece + turn, pieces)
        zs = [near * per_piece + i for i in range(per_piece)]
        if turn == pieces - 1:
            ex.relay(True, ex.depth - 1)
        columns(2 * ex.y + ex.c, near)
        ex.beside(True, ex.y, zs)
        columns(2 * ex.y + 1 - ex.c, near)
        for z in zs:
            ex.crossed(True, z)
        columns(2 * (1 - ex.y) + ex.c, near)
        ex.beside(True, 1 - ex.y, zs)
        columns(2 * (1 - ex.y) + 1 - ex.c, near)
    for piece in range(kept.shape[0]):
        part(piece).wait_recv()
    blocks = [kept[piece] + came[piece] for piece in range(kept.shape[0])]
    updated = tokens[...].astype(jnp.float32) + jnp.concatenate(blocks, axis=1)

    def finish():
        token_copy.wait_send()
        for piece in range(kept.shape[0]):
            part(piece).wait_send()
        ex.finish()

    return updated, finish


def splat(held, slots, total, bins, sources, between):
    half = total.shape[0]
    tokens = held.shape[2]
    chunks = slots.shape[2] // CHUNK
    total[...] = jnp.zeros_like(total)

    def one_source(source):
        def step(i, inner):
            start = pl.multiple_of(i * CHUNK, CHUNK)
            packed = slots[source, :, pl.ds(start, CHUNK)]
            point, cell = packed // 65536, packed % 65536
            token, depth_bin = point // bins, point % bins
            token_ids = lax.broadcasted_iota(jnp.int32, (tokens, CHUNK), 0)
            pick = jnp.where(token_ids == token, 1.0, 0.0).astype(jnp.bfloat16)
            got = jnp.dot(held[source], pick, preferred_element_type=jnp.float32)
            bin_ids = lax.broadcasted_iota(jnp.int32, (bins, CHUNK), 0)
            weight = jnp.sum(
                jnp.where(bin_ids == depth_bin, got[:bins], 0.0), axis=0, keepdims=True
            )
            upper = cell >= half
            low = jnp.where(upper, 0.0, weight) * got[bins:]
            high = jnp.where(upper, weight, 0.0) * got[bins:]
            lifted = jnp.concatenate([low, high], axis=0).astype(jnp.bfloat16)
            local = jnp.where(upper, cell - half, cell)
            cell_ids = lax.broadcasted_iota(jnp.int32, (half, CHUNK), 0)
            place = jnp.where(cell_ids == local, 1.0, 0.0).astype(jnp.bfloat16)
            total[...] += lax.dot_general(
                place, lifted, (((1,), (1,)), ((), ())), preferred_element_type=jnp.float32
            )
            return inner

        lax.fori_loop(0, chunks, step, 0)

    for turn, source in enumerate(sources):
        between(turn, source)
        one_source(source)


class Tables:
    def __init__(self, tiles, table, held, sends, recv):
        self.cam, self.tile = lax.axis_index("cam"), lax.axis_index("tile")
        self.depth = tiles // 2
        self.z, self.x = self.tile // 2, lax.rem(self.tile, 2)
        self.table, self.held, self.recv = table, held, recv
        self.up, self.down, self.pair = sends

    def to(self, route, z):
        source = 2 * z + self.x
        dst = self.held.at[source]
        src = dst
        got = self.recv.at[source]
        if route == "up":
            return remote(src, dst, self.up.at[z], got, self.cam, self.tile + 2)
        if route == "down":
            return remote(src, dst, self.down.at[z], got, self.cam, self.tile - 2)
        return remote(src, dst, self.pair.at[z], got, self.cam, self.tile + 1 - 2 * self.x)

    def wait(self, source):
        dst = self.held.at[source]
        remote(dst, dst, self.pair.at[0], self.recv.at[source], self.cam, self.tile).wait_recv()

    def begin(self):
        pl.when(self.z + 1 < self.depth)(lambda: self.to("up", self.z).start())
        pl.when(self.z > 0)(lambda: self.to("down", self.z).start())
        self.to("pair", self.z).start()

    def relay(self, d):
        def take(z, more, route):
            self.wait(2 * z + self.x)
            pl.when(more)(lambda: self.to(route, z).start())
            self.to("pair", z).start()

        up, down = self.z + 1 < self.depth, self.z > 0
        pl.when(self.z - d >= 0)(lambda: take(self.z - d, up, "up"))
        pl.when(self.z + d < self.depth)(lambda: take(self.z + d, down, "down"))

    def place(self, turn):
        if self.depth & (self.depth - 1) == 0:
            return self.z ^ turn
        return lax.rem(self.z + turn, self.depth)

    def sources(self):
        found = []
        for turn in range(self.depth):
            found += [2 * self.place(turn) + self.x, 2 * self.place(turn) + 1 - self.x]
        return found

    def between(self, turn, source):
        if 0 < turn < self.depth:
            self.relay(turn)
        if turn % 2 == 1:
            self.wait(source)

    def finish(self):
        for z in range(self.depth):
            up = (self.z >= z) & (self.z + 1 < self.depth)
            pl.when(up)(lambda: self.to("up", z).wait_send())
            pl.when((self.z <= z) & (self.z > 0))(lambda: self.to("down", z).wait_send())
            self.to("pair", z).wait_send()


def fill_slots(point, cell, count, slots, points):
    tiles, _, width = slots.shape
    used = point.shape[2]
    ids = lax.broadcasted_iota(jnp.int32, (1, used), 1)
    for k in range(tiles):
        if used < width:
            slots[k] = jnp.full((1, width), points * 65536, jnp.int32)
        live = ids < count[0, k]
        row = jnp.where(live, point[0, k : k + 1, :], points) * 65536
        slots[k, :, :used] = row + cell[0, k : k + 1, :]


def fill_own(gate, up, down, own):
    units = gate.shape[1]
    width = own.shape[3]
    even = units - units % LANES
    for half in range(2):
        first = half * width
        full = min(width, even - first)
        for which, ref in ((0, gate), (1, up), (2, None)):

            def taken(start, size):
                if ref is None:
                    rows = down[start : start + size, :].astype(jnp.float32)
                    return jnp.transpose(rows).astype(jnp.bfloat16)
                return ref[:, start : start + size]

            own[half, which, :, :full] = taken(first, full)
            if full < width:
                rest = units - first - full
                blank = jnp.zeros((own.shape[2], width - full), jnp.bfloat16)
                own[half, which, :, full:] = blank
                if rest > 0:
                    own[half, which, :, full : full + rest] = taken(first + full, rest)


def widen(source, index, wide, row):
    value = source[index].astype(jnp.float32)
    columns, channels = value.shape
    places = lax.broadcasted_iota(jnp.int32, (columns, channels), 0)
    left = jnp.where(places == 0, 0.0, pltpu.roll(value, 1, 0))
    right = jnp.where(places == columns - 1, 0.0, pltpu.roll(value, columns - 1, 0))
    wide[row] = jnp.concatenate([left, value, right], axis=1).astype(jnp.bfloat16)


def convolve(wide, row, weight):
    total = None
    for shift in range(3):
        taps = weight[shift].reshape(wide.shape[2], -1)
        got = jnp.dot(wide[row + shift], taps, preferred_element_type=jnp.float32)
        total = got if total is None else total + got
    return total


def program(fused, tiles, bins, *refs):
    if fused:
        (tokens, gain, w_gate, w_up, w_down, head_gain, w_depth, w_context) = refs[:8]
        (point, cell, live, w1, b1, w2, b2, out) = refs[8:16]
        refs = refs[16:]
    else:
        (table_in, point, cell, live, w1, b1, w2, b2, out) = refs[:9]
        refs = refs[9:]
    (slot_in, slots, held, total, ext, wide, mid, wide_mid) = refs[:8]
    (slot_send, slot_recv, t_up, t_down, t_pair, t_recv, halo_send, halo_recv) = refs[8:16]
    if fused:
        (own, whole, guest, normed, gate, up, hidden, kept, sent, came) = refs[16:26]
        (recv, zup, zdown, side, core, pair) = refs[26:32]
        sems = refs[32:37]
    cam, me = lax.axis_index("cam"), lax.axis_index("tile")
    token_count = held.shape[2]
    barrier = pltpu.get_barrier_semaphore()

    def hello(other_cam, other_tile):
        pl.semaphore_signal(
            barrier, inc=1, device_id={"cam": other_cam, "tile": other_tile}, device_id_type=MESH
        )

    if fused:
        y, c = cam // 2, lax.rem(cam, 2)
        before, after = me >= 2, me + 2 < tiles
        hello(2 * y + 1 - c, me)
        hello(2 * (1 - y) + c, me)
        hello(cam, me + 1 - 2 * lax.rem(me, 2))
        pl.when(before)(lambda: hello(cam, me - 2))
        pl.when(after)(lambda: hello(cam, me + 2))
        expected = 3 + jnp.where(before, 1, 0) + jnp.where(after, 1, 0)
        fill_own(w_gate, w_up, w_down, own)
        normed[:token_count] = layer_norm(tokens[...].astype(jnp.float32), gain[...]).astype(
            jnp.bfloat16
        )
    else:

        def greet(k, carry):
            hello(cam, lax.rem(me + k, tiles))
            return carry

        lax.fori_loop(1, tiles, greet, 0)
        expected = tiles - 1
    fill_slots(point, cell, live, slot_in, token_count * bins)
    pl.semaphore_wait(barrier, expected)

    def slot_copy(k):
        other = lax.rem(me + k, tiles)
        return remote(slot_in.at[other], slots.at[me], slot_send.at[k], slot_recv.at[k], cam, other)

    def slot_wait(k):
        source = lax.rem(me - k + tiles, tiles)
        remote(
            slot_in.at[me], slots.at[source], slot_send.at[k], slot_recv.at[k], cam, me
        ).wait_recv()

    def slot_start(k, carry):
        slot_copy(k).start()
        return carry

    def slot_finish(k, carry):
        slot_wait(k)
        slot_copy(k).wait_send()
        return carry

    own_slots = pltpu.make_async_copy(slot_in.at[me], slots.at[me], slot_send.at[0])

    def send_slots():
        lax.fori_loop(1, tiles, slot_start, 0)
        own_slots.start()

    if fused:
        ex = Exchange(tiles, own, whole, recv, (zup, zdown, side, core, pair))
        updated, finish = feed_forward(
            ex, tokens, gain, guest, normed, gate, up, hidden, kept, sent, came, sems, send_slots
        )
        head_input = layer_norm(updated, head_gain[...]).astype(jnp.bfloat16)
        scores = [
            jnp.transpose(jnp.dot(head_input, weight[...], preferred_element_type=jnp.float32))
            for weight in (w_depth, w_context)
        ]
        held[me] = soft_table(jnp.concatenate(scores, axis=0), bins)
    else:
        send_slots()
        held[me] = table_in[...]
    tables = Tables(tiles, None, held, (t_up, t_down, t_pair), t_recv)
    tables.begin()
    own_slots.wait()
    lax.fori_loop(1, tiles, slot_finish, 0)
    splat(held, slots, total, bins, tables.sources(), tables.between)
    channels = total.shape[1] // 2
    per_scene = ROWS_DEV * GRID_W
    for scene in range(SCN):
        for row in range(ROWS_DEV):
            start = scene * per_scene + row * GRID_W
            side_of, first = divmod(start, total.shape[0])
            ext[scene, 2 + row] = total[
                first : first + GRID_W, side_of * channels : (side_of + 1) * channels
            ].astype(jnp.bfloat16)

    def halo(which):
        if which == 0:
            src, dst, other = ext.at[:, 2:4], ext.at[:, ROWS_DEV + 2 : ROWS_DEV + 4], me - 1
        else:
            src, dst, other = ext.at[:, ROWS_DEV : ROWS_DEV + 2], ext.at[:, 0:2], me + 1
        return remote(src, dst, halo_send.at[which], halo_recv.at[which], cam, other)

    blank = jnp.zeros((SCN, 2, GRID_W, channels), jnp.bfloat16)

    def first_tile():
        ext[:, 0:2] = blank

    def last_tile():
        ext[:, ROWS_DEV + 2 : ROWS_DEV + 4] = blank

    has_before, has_after = me > 0, me + 1 < tiles
    pl.when(has_before)(lambda: halo(0).start())
    pl.when(has_after)(lambda: halo(1).start())
    pl.when(me == 0)(first_tile)
    pl.when(me + 1 == tiles)(last_tile)
    rows_ext = ROWS_DEV + 4
    for scene in range(SCN):
        for row in range(2, ROWS_DEV + 2):
            widen(ext, (scene, row), wide, scene * rows_ext + row)
    pl.when(has_before)(lambda: halo(1).wait_recv())
    pl.when(has_after)(lambda: halo(0).wait_recv())
    for scene in range(SCN):
        for row in (0, 1, ROWS_DEV + 2, ROWS_DEV + 3):
            widen(ext, (scene, row), wide, scene * rows_ext + row)
    rows_mid = ROWS_DEV + 2
    for scene in range(SCN):
        for row in range(rows_mid):
            value = jnp.maximum(convolve(wide, scene * rows_ext + row, w1) + b1[...], 0.0)
            if row == 0:
                value = jnp.where(has_before, value, 0.0)
            if row == rows_mid - 1:
                value = jnp.where(has_after, value, 0.0)
            mid[scene, row] = value.astype(jnp.bfloat16)
            widen(mid, (scene, row), wide_mid, scene * rows_mid + row)
    for scene in range(SCN):
        for row in range(ROWS_DEV):
            value = convolve(wide_mid, scene * rows_mid + row, w2) + b2[...]
            value = ext[scene, 2 + row].astype(jnp.float32) + value
            out[scene, row] = value.astype(jnp.bfloat16)
    pl.when(has_before)(lambda: halo(0).wait_send())
    pl.when(has_after)(lambda: halo(1).wait_send())
    tables.finish()
    if fused:
        finish()


def run(fused, arrays, slots, weights, sizes):
    tiles, bins, channels, token_count = sizes
    cells = SCN * ROWS_DEV * GRID_W
    dma = pltpu.SemaphoreType.DMA
    bf16, f32 = jnp.bfloat16, jnp.float32
    slot_count = slots[0].shape[2]
    slot_width = slot_count + -slot_count % CHUNK
    scratch = [
        pltpu.VMEM((tiles, 1, slot_width), jnp.int32),
        pltpu.VMEM((tiles, 1, slot_width), jnp.int32),
        pltpu.VMEM((tiles, bins + channels, token_count), bf16),
        pltpu.VMEM((cells // 2, 2 * channels), f32),
        pltpu.VMEM((SCN, ROWS_DEV + 4, GRID_W, channels), bf16),
        pltpu.VMEM((SCN * (ROWS_DEV + 4), GRID_W, 3 * channels), bf16),
        pltpu.VMEM((SCN, ROWS_DEV + 2, GRID_W, channels), bf16),
        pltpu.VMEM((SCN * (ROWS_DEV + 2), GRID_W, 3 * channels), bf16),
        dma((tiles,)),
        dma((tiles,)),
        dma((tiles // 2,)),
        dma((tiles // 2,)),
        dma((tiles // 2,)),
        dma((tiles,)),
        dma((2,)),
        dma((2,)),
    ]
    operands = [*arrays, *slots, *weights]
    specs = [pl.BlockSpec(memory_space=pltpu.VMEM)] * len(operands)
    specs[len(arrays) + 2] = pl.BlockSpec(memory_space=pltpu.SMEM)
    if fused:
        tokens, gate_weight = arrays[0], arrays[2]
        count, width = tokens.shape
        rows, units = gate_weight.shape
        cams = lax.axis_size("cam")
        half = (units + -units % (2 * LANES)) // 2
        pieces = width // LANES
        scratch += [
            pltpu.VMEM((2, 3, rows, half), bf16),
            pltpu.VMEM((3, width, half), bf16),
            pltpu.VMEM((count, width), bf16),
            pltpu.VMEM((2 * count, width), bf16),
            pltpu.VMEM((2 * count, half), f32),
            pltpu.VMEM((2 * count, half), f32),
            pltpu.VMEM((2 * count, half), bf16),
            pltpu.VMEM((pieces, count, LANES), f32),
            pltpu.VMEM((pieces, count, LANES), f32),
            pltpu.VMEM((pieces, count, LANES), f32),
            dma((4, cams * tiles)),
            dma((4, 2, tiles)),
            dma((4, 2, tiles)),
            dma((4, 2, tiles)),
            dma((4, 2, tiles)),
            dma((4,)),
            dma((2,)),
            dma,
            dma,
            dma((pieces,)),
            dma((pieces,)),
        ]
    return pl.pallas_call(
        functools.partial(program, fused, tiles, bins),
        out_shape=jax.ShapeDtypeStruct((SCN, ROWS_DEV, GRID_W, channels), bf16),
        in_specs=specs,
        out_specs=pl.BlockSpec(memory_space=pltpu.VMEM),
        scratch_shapes=scratch,
        compiler_params=pltpu.CompilerParams(
            collective_id=0, has_side_effects=True, vmem_limit_bytes=60 * 1024 * 1024
        ),
    )(*operands)


def table_of(tokens, ln_gain, gate_weight, up_weight, down_weight, head_gain, head):
    inputs = tokens.astype(jnp.float32)
    normed = layer_norm(inputs, ln_gain).astype(jnp.bfloat16)
    axes = ("cam", "tile")
    gate_whole = lax.all_gather(gate_weight, axes, axis=0, tiled=True)
    up_whole = lax.all_gather(up_weight, axes, axis=0, tiled=True)
    gate = jnp.dot(normed, gate_whole, preferred_element_type=jnp.float32)
    up = jnp.dot(normed, up_whole, preferred_element_type=jnp.float32)
    hidden = (jax.nn.silu(gate) * up).astype(jnp.bfloat16)
    down_whole = lax.all_gather(down_weight.T, axes, axis=0, tiled=True)
    contract = (((1,), (1,)), ((), ()))
    branch = lax.dot_general(hidden, down_whole, contract, preferred_element_type=jnp.float32)
    head_input = layer_norm(inputs + branch, head_gain).astype(jnp.bfloat16)
    return lax.dot_general(head, head_input, contract, preferred_element_type=jnp.float32)


def on_device(
    tokens,
    ln_gain,
    gate_weight,
    up_weight,
    down_weight,
    head_gain,
    depth_weight,
    context_weight,
    slot_point,
    slot_cell,
    slot_count,
    conv1_weight,
    conv1_bias,
    conv2_weight,
    conv2_bias,
):
    tiles, cams = lax.axis_size("tile"), lax.axis_size("cam")
    token_count, width = tokens.shape
    bins, channels = depth_weight.shape[1], context_weight.shape[1]
    slots = [slot_point, slot_cell, slot_count]
    weights = [
        conv1_weight,
        conv1_bias.reshape(1, channels),
        conv2_weight,
        conv2_bias.reshape(1, channels),
    ]
    sizes = (tiles, bins, channels, token_count)
    rows, units = gate_weight.shape
    fused = cams == 4 and tiles % 4 == 0 and rows % 16 == 0 and (rows * tiles) % LANES == 0
    if not fused:
        head = jnp.concatenate([depth_weight, context_weight], axis=1).T
        scores = table_of(
            tokens, ln_gain, gate_weight, up_weight, down_weight, head_gain, head
        )
        return run(False, [soft_table(scores, bins)], slots, weights, sizes)
    arrays = [
        tokens,
        ln_gain.reshape(1, width),
        gate_weight,
        up_weight,
        down_weight,
        head_gain.reshape(1, width),
        depth_weight,
        context_weight,
    ]
    return run(True, arrays, slots, weights, sizes)


def solution(mesh):
    return jax.shard_map(
        on_device,
        mesh=mesh,
        in_specs=(
            P(("cam", "tile"), None),
            P(),
            P(("cam", "tile"), None),
            P(("cam", "tile"), None),
            P(None, ("cam", "tile")),
            P(),
            P(),
            P(),
            P(("cam", "tile"), None, None),
            P(("cam", "tile"), None, None),
            P(("cam", "tile"), None),
            P(),
            P(),
            P(),
            P(),
        ),
        out_specs=P("cam", "tile", None, None),
        check_vma=False,
    )
```

```python
import functools

import jax
import jax.numpy as jnp
from jax import lax
from jax.experimental import pallas as pl
from jax.experimental.pallas import tpu as pltpu
from jax.sharding import PartitionSpec as P

ROWS_DEV = 4
GRID_W = 256
SCN = 2
LANES = 128
MESH = pl.DeviceIdType.MESH


def layer_norm(values, gain):
    center = values - jnp.mean(values, axis=-1, keepdims=True)
    spread = jnp.mean(center * center, axis=-1, keepdims=True)
    return center * lax.rsqrt(spread + 1e-06) * gain


def remote(src, dst, send, recv, cam, tile):
    return pltpu.make_async_remote_copy(
        src_ref=src,
        dst_ref=dst,
        send_sem=send,
        recv_sem=recv,
        device_id={"cam": cam, "tile": tile},
        device_id_type=MESH,
    )


def soft_depth(logits):
    raised = jnp.exp(logits - jnp.max(logits, axis=0, keepdims=True))
    return raised / jnp.sum(raised, axis=0, keepdims=True)


def table_of(depth, context):
    bins, tokens = depth.shape
    rows = [context.astype(jnp.bfloat16)]
    depth = depth.astype(jnp.bfloat16)
    for first in range(0, tokens, LANES):
        block = depth[:, first : first + LANES]
        if block.shape[1] < LANES:
            blank = jnp.zeros((bins, LANES - block.shape[1]), jnp.bfloat16)
            block = jnp.concatenate([block, blank], axis=1)
        rows.append(block)
    return jnp.concatenate(rows, axis=0)


class Exchange:
    SPAN = ((0, 1), (1, 1), (2, 1), (0, 2))

    def __init__(self, tiles, own, whole, recv, sends):
        self.cam, self.tile = lax.axis_index("cam"), lax.axis_index("tile")
        self.tiles, self.depth = tiles, tiles // 2
        self.y, self.c = self.cam // 2, lax.rem(self.cam, 2)
        self.z, self.x = self.tile // 2, lax.rem(self.tile, 2)
        self.own, self.whole, self.recv = own, whole, recv
        self.up, self.down, self.side, self.core, self.pair = sends
        self.rows = own.shape[2]

    def shard(self, y, c, z, x):
        return (2 * y + c) * self.tiles + 2 * z + x

    def block(self, kind, shard):
        first, count = self.SPAN[kind]
        rows = pl.ds(pl.multiple_of(shard * self.rows, self.rows), self.rows)
        return self.whole.at[pl.ds(first, count), rows, :]

    def mine(self, kind, half):
        first, count = self.SPAN[kind]
        return self.own.at[half, pl.ds(first, count)]

    def to(self, route, kind, y, z, x):
        shard = self.shard(y, self.c, z, x)
        block = self.block(kind, shard)
        at = (kind, y, 2 * z + x)
        got = self.recv.at[kind, shard]
        if route == "up":
            return remote(block, block, self.up.at[at], got, self.cam, self.tile + 2)
        if route == "down":
            return remote(block, block, self.down.at[at], got, self.cam, self.tile - 2)
        if route == "side":
            other = 2 * (1 - self.y) + self.c
            return remote(block, block, self.side.at[at], got, other, self.tile)
        other = 2 * self.y + 1 - self.c
        return remote(block, block, self.core.at[at], got, other, self.tile)

    def across(self, kind):
        shard = self.shard(self.y, self.c, self.z, self.x)
        return remote(
            self.mine(kind, 1 - self.x),
            self.block(kind, shard),
            self.pair.at[kind],
            self.recv.at[kind, shard],
            self.cam,
            self.tile + 1 - 2 * self.x,
        )

    def wait(self, kind, y, c, z, x):
        shard = self.shard(y, c, z, x)
        block = self.block(kind, shard)
        remote(
            block, block, self.pair.at[kind], self.recv.at[kind, shard], self.cam, self.tile
        ).wait_recv()

    def spread(self, kind, y, x, side):
        def go_up():
            self.to("up", kind, y, self.z, x).start()

        def go_down():
            self.to("down", kind, y, self.z, x).start()

        if side:
            self.to("side", kind, y, self.z, x).start()
        pl.when(self.z + 1 < self.depth)(go_up)
        pl.when(self.z > 0)(go_down)
        self.to("core", kind, y, self.z, x).start()

    def units(self, late):
        mate = 1 - self.x
        if late:
            return ((2, self.y, self.x, True), (2, self.y, mate, True))
        return (
            (0, self.y, self.x, True),
            (1, self.y, self.x, False),
            (1, 1 - self.y, self.x, False),
            (3, self.y, mate, True),
        )

    def relay(self, late, d):
        def take(kind, y, z, x, side, more, route):
            self.wait(kind, y, self.c, z, x)
            if d + 1 < self.depth:
                pl.when(more)(lambda: self.to(route, kind, y, z, x).start())
            if side:
                self.to("side", kind, y, z, x).start()
            self.to("core", kind, y, z, x).start()

        for kind, y, x, side in self.units(late):

            def below():
                take(kind, y, self.z - d, x, side, self.z + 1 < self.depth, "up")

            def above():
                take(kind, y, self.z + d, x, side, self.z > 0, "down")

            pl.when(self.z - d >= 0)(below)
            pl.when(self.z + d < self.depth)(above)

    def crossed(self, late, z):
        for kind, y, x, side in self.units(late):
            if side:
                self.wait(kind, 1 - self.y, self.c, z, x)
                self.to("core", kind, 1 - self.y, z, x).start()

    def crossed_at(self, late, d):
        pl.when(self.z - d >= 0)(lambda: self.crossed(late, self.z - d))
        pl.when(self.z + d < self.depth)(lambda: self.crossed(late, self.z + d))

    def beside(self, late, y, zs):
        for z in zs:
            if late:
                for x in range(2):
                    self.wait(2, y, 1 - self.c, z, x)
            else:
                self.wait(0, y, 1 - self.c, z, self.x)
                self.wait(1, y, 1 - self.c, z, self.x)
                self.wait(3, y, 1 - self.c, z, 1 - self.x)

    def finish(self):
        self.across(3).wait_send()
        self.across(2).wait_send()
        for z in range(self.depth):
            for kind, y, x, side in (*self.units(False), *self.units(True)):

                def up():
                    self.to("up", kind, y, z, x).wait_send()

                def down():
                    self.to("down", kind, y, z, x).wait_send()

                pl.when((self.z >= z) & (self.z + 1 < self.depth))(up)
                pl.when((self.z <= z) & (self.z > 0))(down)
                self.to("core", kind, y, z, x).wait_send()
                if side:
                    self.to("side", kind, y, z, x).wait_send()
                    self.to("core", kind, 1 - y, z, x).wait_send()
        self.to("side", 1, self.y, self.z, self.x).wait_send()


def feed_forward(ex, tokens, gain, guest, normed, gate, up, hidden, kept, sent, came, sems, midway):
    local, tok_send, tok_recv, part_send, part_recv = sems
    count = tokens.shape[0]
    mate = ex.tile + 1 - 2 * ex.x
    token_copy = remote(tokens, guest, tok_send, tok_recv, ex.cam, mate)
    me = ex.shard(ex.y, ex.c, ex.z, ex.x)
    copies = [
        pltpu.make_async_copy(ex.mine(kind, ex.x), ex.block(kind, me), local.at[kind - 2])
        for kind in (3, 2)
    ]
    ex.across(3).start()
    for copy in copies:
        copy.start()
    copies[0].wait()
    ex.to("side", 1, ex.y, ex.z, ex.x).start()
    ex.spread(0, ex.y, ex.x, True)
    ex.spread(1, ex.y, ex.x, False)
    ex.across(2).start()
    token_copy.start()
    ex.wait(1, 1 - ex.y, ex.c, ex.z, ex.x)
    ex.spread(1, 1 - ex.y, ex.x, False)
    ex.wait(3, ex.y, ex.c, ex.z, 1 - ex.x)
    ex.spread(3, ex.y, 1 - ex.x, True)
    ex.relay(False, 1)
    ex.crossed(False, ex.z)
    for d in range(2, ex.depth - 1):
        ex.relay(False, d)
        ex.crossed_at(False, d - 1)
    copies[1].wait()
    ex.spread(2, ex.y, ex.x, True)
    ex.wait(2, ex.y, ex.c, ex.z, 1 - ex.x)
    ex.spread(2, ex.y, 1 - ex.x, True)
    token_copy.wait_recv()
    normed[count:] = layer_norm(guest[...].astype(jnp.float32), gain[...]).astype(jnp.bfloat16)
    wide = ex.rows * ex.tiles
    pieces = wide // LANES
    per_piece = ex.depth // pieces

    def project(cam, first):
        rows = pl.ds(pl.multiple_of(cam * wide, wide), wide)
        for which, total in ((0, gate), (1, up)):
            got = jnp.dot(
                normed[:, rows], ex.whole[which, rows, :], preferred_element_type=jnp.float32
            )
            if first:
                total[...] = got
            else:
                total[...] += got

    def part(piece):
        return remote(
            sent.at[piece], came.at[piece], part_send.at[piece], part_recv.at[piece], ex.cam, mate
        )

    def columns(cam, near):
        piece = cam * pieces + near
        rows = pl.ds(pl.multiple_of(piece * LANES, LANES), LANES)
        got = lax.dot_general(
            hidden[...],
            ex.whole[2, rows, :],
            (((1,), (1,)), ((), ())),
            preferred_element_type=jnp.float32,
        )
        kept[piece] = got[:count]
        sent[piece] = got[count:]
        part(piece).start()

    every = range(ex.depth)
    ex.relay(False, ex.depth - 1)
    midway()
    project(2 * ex.y + ex.c, True)
    ex.crossed_at(False, ex.depth - 2)
    ex.relay(True, 1)
    ex.beside(False, ex.y, every)
    project(2 * ex.y + 1 - ex.c, False)
    ex.crossed_at(False, ex.depth - 1)
    project(2 * (1 - ex.y) + ex.c, False)
    for d in range(2, ex.depth - 1):
        ex.relay(True, d)
    ex.beside(False, 1 - ex.y, every)
    project(2 * (1 - ex.y) + 1 - ex.c, False)
    value = gate[...]
    hidden[...] = (value / (1.0 + jnp.exp(-value)) * up[...]).astype(jnp.bfloat16)
    for turn in range(pieces):
        near = lax.rem(ex.z // per_piece + turn, pieces)
        zs = [near * per_piece + i for i in range(per_piece)]
        if turn == pieces - 1:
            ex.relay(True, ex.depth - 1)
        columns(2 * ex.y + ex.c, near)
        ex.beside(True, ex.y, zs)
        columns(2 * ex.y + 1 - ex.c, near)
        for z in zs:
            ex.crossed(True, z)
        columns(2 * (1 - ex.y) + ex.c, near)
        ex.beside(True, 1 - ex.y, zs)
        columns(2 * (1 - ex.y) + 1 - ex.c, near)
    for piece in range(kept.shape[0]):
        part(piece).wait_recv()
    blocks = [kept[piece] + came[piece] for piece in range(kept.shape[0])]
    updated = tokens[...].astype(jnp.float32) + jnp.concatenate(blocks, axis=1)

    def finish():
        token_copy.wait_send()
        for piece in range(kept.shape[0]):
            part(piece).wait_send()
        ex.finish()

    return updated, finish


def one_hot(count, index):
    ids = lax.broadcasted_iota(jnp.int16, (count, index.shape[1]), 0)
    one, zero = jnp.array(1, jnp.bfloat16), jnp.array(0, jnp.bfloat16)
    return jnp.where(ids == index.astype(jnp.int16), one, zero)


def lift(table, packed, tokens, bins):
    point = packed // 65536
    token, depth_bin = point // bins, point % bins
    pick = one_hot(tokens, token)
    blocks = []
    for first in range(0, tokens, LANES):
        row = tokens + first // LANES * bins
        blocks.append(table[row : row + bins, : min(LANES, tokens - first)])
    depth = jnp.concatenate(blocks, axis=1)
    found = jnp.dot(depth, pick, preferred_element_type=jnp.float32)
    bin_ids = lax.broadcasted_iota(jnp.int32, found.shape, 0)
    weight = jnp.sum(jnp.where(bin_ids == depth_bin, found, 0.0), axis=0, keepdims=True)
    context = lax.dot_general(
        table[:tokens], pick, (((0,), (0,)), ((), ())), preferred_element_type=jnp.float32
    )
    return weight * context


def add_scene(total, scene, lifted, packed):
    half = total.shape[1]
    cell = packed % 65536
    part = cell // half
    low = jnp.where(part == 2 * scene, lifted, 0.0)
    high = jnp.where(part == 2 * scene + 1, lifted, 0.0)
    both = jnp.concatenate([low, high], axis=0).astype(jnp.bfloat16)
    place = one_hot(half, cell % half)
    total[scene] += lax.dot_general(
        place, both, (((1,), (1,)), ((), ())), preferred_element_type=jnp.float32
    )


class Tables:
    def __init__(self, tiles, held, sends, recv):
        self.cam, self.tile = lax.axis_index("cam"), lax.axis_index("tile")
        self.depth = tiles // 2
        self.z, self.x = self.tile // 2, lax.rem(self.tile, 2)
        self.held, self.recv = held, recv
        self.up, self.down, self.pair = sends

    def to(self, route, z):
        source = 2 * z + self.x
        dst = self.held.at[source]
        src = dst
        got = self.recv.at[source]
        if route == "up":
            return remote(src, dst, self.up.at[z], got, self.cam, self.tile + 2)
        if route == "down":
            return remote(src, dst, self.down.at[z], got, self.cam, self.tile - 2)
        return remote(src, dst, self.pair.at[z], got, self.cam, self.tile + 1 - 2 * self.x)

    def wait(self, source):
        dst = self.held.at[source]
        remote(dst, dst, self.pair.at[0], self.recv.at[source], self.cam, self.tile).wait_recv()

    def begin(self):
        pl.when(self.z + 1 < self.depth)(lambda: self.to("up", self.z).start())
        pl.when(self.z > 0)(lambda: self.to("down", self.z).start())
        self.to("pair", self.z).start()

    def relay(self, d):
        def take(z, more, route):
            self.wait(2 * z + self.x)
            pl.when(more)(lambda: self.to(route, z).start())
            self.to("pair", z).start()

        up, down = self.z + 1 < self.depth, self.z > 0
        pl.when(self.z - d >= 0)(lambda: take(self.z - d, up, "up"))
        pl.when(self.z + d < self.depth)(lambda: take(self.z + d, down, "down"))

    def source(self, turn):
        step = turn // 2
        if self.depth & (self.depth - 1) == 0:
            z = self.z ^ step
        else:
            z = lax.rem(self.z + step, self.depth)
        return 2 * z + (self.x ^ lax.rem(turn, 2))

    def between(self, turn):
        pl.when((turn > 0) & (turn < self.depth))(lambda: self.relay(turn))
        pl.when(lax.rem(turn, 2) == 1)(lambda: self.wait(self.source(turn)))

    def finish(self):
        for z in range(self.depth):
            up = (self.z >= z) & (self.z + 1 < self.depth)
            pl.when(up)(lambda: self.to("up", z).wait_send())
            pl.when((self.z <= z) & (self.z > 0))(lambda: self.to("down", z).wait_send())
            self.to("pair", z).wait_send()


def fill_slots(point, cell, count, slots, points):
    tiles, _, width = slots.shape
    used = point.shape[2]
    ids = lax.broadcasted_iota(jnp.int32, (1, used), 1)
    for k in range(tiles):
        if used < width:
            slots[k] = jnp.full((1, width), points * 65536, jnp.int32)
        live = ids < count[0, k]
        row = jnp.where(live, point[0, k : k + 1, :], points) * 65536
        slots[k, :, :used] = row + cell[0, k : k + 1, :]


def fill_own(gate, up, down, own):
    units = gate.shape[1]
    width = own.shape[3]
    even = units - units % LANES
    for half in range(2):
        first = half * width
        full = min(width, even - first)
        for which, ref in ((0, gate), (1, up), (2, down)):
            own[half, which, :, :full] = ref[:, first : first + full]
            if full < width:
                rest = units - first - full
                blank = jnp.zeros((own.shape[2], width - full), jnp.bfloat16)
                own[half, which, :, full:] = blank
                if rest > 0:
                    tail = ref[:, first + full : units]
                    own[half, which, :, full : full + rest] = tail


def widen(source, index, wide, row):
    value = source[index].astype(jnp.float32)
    columns, channels = value.shape
    places = lax.broadcasted_iota(jnp.int32, (columns, channels), 0)
    left = jnp.where(places == 0, 0.0, pltpu.roll(value, 1, 0))
    right = jnp.where(places == columns - 1, 0.0, pltpu.roll(value, columns - 1, 0))
    wide[row] = jnp.concatenate([left, value, right], axis=1).astype(jnp.bfloat16)


def convolve(wide, row, weight):
    total = None
    for shift in range(3):
        taps = weight[shift].reshape(wide.shape[2], -1)
        got = jnp.dot(wide[row + shift], taps, preferred_element_type=jnp.float32)
        total = got if total is None else total + got
    return total


def program(fused, tiles, bins, token_count, *refs):
    if fused:
        (tokens, gain, w_gate, w_up, w_down, head_gain, w_depth, w_context) = refs[:8]
        (point, cell, live, w1, b1, w2, b2, out) = refs[8:16]
        refs = refs[16:]
    else:
        (table_in, point, cell, live, w1, b1, w2, b2, out) = refs[:9]
        refs = refs[9:]
    (slot_in, slots, held, lifted, total, ext, wide, mid, wide_mid) = refs[:9]
    (slot_send, slot_recv, t_up, t_down, t_pair, t_recv, halo_send, halo_recv) = refs[9:17]
    if fused:
        (own, whole, guest, normed, gate, up, hidden, kept, sent, came) = refs[17:27]
        (recv, zup, zdown, side, core, pair) = refs[27:33]
        sems = refs[33:38]
    cam, me = lax.axis_index("cam"), lax.axis_index("tile")
    barrier = pltpu.get_barrier_semaphore()

    def hello(other_cam, other_tile):
        pl.semaphore_signal(
            barrier, inc=1, device_id={"cam": other_cam, "tile": other_tile}, device_id_type=MESH
        )

    if fused:
        y, c = cam // 2, lax.rem(cam, 2)
        before, after = me >= 2, me + 2 < tiles
        hello(2 * y + 1 - c, me)
        hello(2 * (1 - y) + c, me)
        hello(cam, me + 1 - 2 * lax.rem(me, 2))
        pl.when(before)(lambda: hello(cam, me - 2))
        pl.when(after)(lambda: hello(cam, me + 2))
        expected = 3 + jnp.where(before, 1, 0) + jnp.where(after, 1, 0)
        fill_own(w_gate, w_up, w_down, own)
        normed[:token_count] = layer_norm(tokens[...].astype(jnp.float32), gain[...]).astype(
            jnp.bfloat16
        )
    else:

        def greet(k, carry):
            hello(cam, lax.rem(me + k, tiles))
            return carry

        lax.fori_loop(1, tiles, greet, 0)
        expected = tiles - 1
    fill_slots(point, cell, live, slot_in, token_count * bins)
    pl.semaphore_wait(barrier, expected)

    def slot_copy(k):
        other = lax.rem(me + k, tiles)
        return remote(slot_in.at[other], slots.at[me], slot_send.at[k], slot_recv.at[k], cam, other)

    def slot_wait(k):
        source = lax.rem(me - k + tiles, tiles)
        remote(
            slot_in.at[me], slots.at[source], slot_send.at[k], slot_recv.at[k], cam, me
        ).wait_recv()

    def slot_start(k, carry):
        slot_copy(k).start()
        return carry

    def slot_finish(k, carry):
        slot_wait(k)
        slot_copy(k).wait_send()
        return carry

    own_slots = pltpu.make_async_copy(slot_in.at[me], slots.at[me], slot_send.at[0])

    def send_slots():
        lax.fori_loop(1, tiles, slot_start, 0)
        own_slots.start()

    if fused:
        ex = Exchange(tiles, own, whole, recv, (zup, zdown, side, core, pair))
        updated, finish = feed_forward(
            ex, tokens, gain, guest, normed, gate, up, hidden, kept, sent, came, sems, send_slots
        )
        head_input = layer_norm(updated, head_gain[...]).astype(jnp.bfloat16)
        logits = lax.dot_general(
            w_depth[...], head_input, (((1,), (1,)), ((), ())), preferred_element_type=jnp.float32
        )
        context = jnp.dot(head_input, w_context[...], preferred_element_type=jnp.float32)
        held[me] = table_of(soft_depth(logits), context)
    else:
        send_slots()
        held[me] = table_in[...]
    tables = Tables(tiles, held, (t_up, t_down, t_pair), t_recv)
    tables.begin()
    own_slots.wait()
    lax.fori_loop(1, tiles, slot_finish, 0)
    total[...] = jnp.zeros_like(total)
    channels = ext.shape[3]
    rows_ext, rows_mid = ROWS_DEV + 4, ROWS_DEV + 2
    has_before, has_after = me > 0, me + 1 < tiles
    blank = jnp.zeros((SCN, 2, GRID_W, channels), jnp.bfloat16)

    def first_tile():
        ext[:, 0:2] = blank

    def last_tile():
        ext[:, ROWS_DEV + 2 : ROWS_DEV + 4] = blank

    pl.when(me == 0)(first_tile)
    pl.when(me + 1 == tiles)(last_tile)

    def halo(which, scene):
        if which == 0:
            src, dst, other = ext.at[scene, 2:4], ext.at[scene, ROWS_DEV + 2 : ROWS_DEV + 4], me - 1
        else:
            src, dst, other = ext.at[scene, ROWS_DEV : ROWS_DEV + 2], ext.at[scene, 0:2], me + 1
        at = (which, scene)
        return remote(src, dst, halo_send.at[at], halo_recv.at[at], cam, other)

    def first_pass(turn, carry):
        tables.between(turn)
        source = tables.source(turn)
        packed = slots[source]
        value = lift(held.at[source], packed, token_count, bins)
        lifted[source] = value.astype(jnp.bfloat16)
        add_scene(total, 0, value, packed)
        return carry

    lax.fori_loop(0, tiles, first_pass, 0)
    for scene in range(SCN):
        if scene > 0:

            def next_pass(source, carry):
                add_scene(total, scene, lifted[source].astype(jnp.float32), slots[source])
                return carry

            lax.fori_loop(0, tiles, next_pass, 0)
        for row in range(ROWS_DEV):
            side_of, first = divmod(row * GRID_W, total.shape[1])
            ext[scene, 2 + row] = total[
                scene, first : first + GRID_W, side_of * channels : (side_of + 1) * channels
            ].astype(jnp.bfloat16)
        pl.when(has_before)(lambda: halo(0, scene).start())
        pl.when(has_after)(lambda: halo(1, scene).start())
    for scene in range(SCN):
        for row in range(2, ROWS_DEV + 2):
            widen(ext, (scene, row), wide, scene * rows_ext + row)
    for scene in range(SCN):
        pl.when(has_before)(lambda: halo(1, scene).wait_recv())
        pl.when(has_after)(lambda: halo(0, scene).wait_recv())
        for row in (0, 1, ROWS_DEV + 2, ROWS_DEV + 3):
            widen(ext, (scene, row), wide, scene * rows_ext + row)
        for row in range(rows_mid):
            value = jnp.maximum(convolve(wide, scene * rows_ext + row, w1) + b1[...], 0.0)
            if row == 0:
                value = jnp.where(has_before, value, 0.0)
            if row == rows_mid - 1:
                value = jnp.where(has_after, value, 0.0)
            mid[scene, row] = value.astype(jnp.bfloat16)
            widen(mid, (scene, row), wide_mid, scene * rows_mid + row)
        for row in range(ROWS_DEV):
            value = convolve(wide_mid, scene * rows_mid + row, w2) + b2[...]
            value = ext[scene, 2 + row].astype(jnp.float32) + value
            out[scene, row] = value.astype(jnp.bfloat16)
    for scene in range(SCN):
        pl.when(has_before)(lambda: halo(0, scene).wait_send())
        pl.when(has_after)(lambda: halo(1, scene).wait_send())
    tables.finish()
    if fused:
        finish()


def run(fused, arrays, slots, weights, sizes):
    tiles, bins, channels, token_count = sizes
    cells = SCN * ROWS_DEV * GRID_W
    dma = pltpu.SemaphoreType.DMA
    bf16, f32 = jnp.bfloat16, jnp.float32
    slot_count = slots[0].shape[2]
    slot_width = slot_count + -slot_count % LANES
    table_rows = token_count + bins * pl.cdiv(token_count, LANES)
    scratch = [
        pltpu.VMEM((tiles, 1, slot_width), jnp.int32),
        pltpu.VMEM((tiles, 1, slot_width), jnp.int32),
        pltpu.VMEM((tiles, table_rows, LANES), bf16),
        pltpu.VMEM((tiles, channels, slot_width), bf16),
        pltpu.VMEM((SCN, cells // SCN // 2, 2 * channels), f32),
        pltpu.VMEM((SCN, ROWS_DEV + 4, GRID_W, channels), bf16),
        pltpu.VMEM((SCN * (ROWS_DEV + 4), GRID_W, 3 * channels), bf16),
        pltpu.VMEM((SCN, ROWS_DEV + 2, GRID_W, channels), bf16),
        pltpu.VMEM((SCN * (ROWS_DEV + 2), GRID_W, 3 * channels), bf16),
        dma((tiles,)),
        dma((tiles,)),
        dma((tiles // 2,)),
        dma((tiles // 2,)),
        dma((tiles // 2,)),
        dma((tiles,)),
        dma((2, SCN)),
        dma((2, SCN)),
    ]
    operands = [*arrays, *slots, *weights]
    specs = [pl.BlockSpec(memory_space=pltpu.VMEM)] * len(operands)
    specs[len(arrays) + 2] = pl.BlockSpec(memory_space=pltpu.SMEM)
    if fused:
        tokens, gate_weight = arrays[0], arrays[2]
        count, width = tokens.shape
        rows, units = gate_weight.shape
        cams = lax.axis_size("cam")
        half = (units + -units % (2 * LANES)) // 2
        pieces = width // LANES
        scratch += [
            pltpu.VMEM((2, 3, rows, half), bf16),
            pltpu.VMEM((3, width, half), bf16),
            pltpu.VMEM((count, width), bf16),
            pltpu.VMEM((2 * count, width), bf16),
            pltpu.VMEM((2 * count, half), f32),
            pltpu.VMEM((2 * count, half), f32),
            pltpu.VMEM((2 * count, half), bf16),
            pltpu.VMEM((pieces, count, LANES), f32),
            pltpu.VMEM((pieces, count, LANES), f32),
            pltpu.VMEM((pieces, count, LANES), f32),
            dma((4, cams * tiles)),
            dma((4, 2, tiles)),
            dma((4, 2, tiles)),
            dma((4, 2, tiles)),
            dma((4, 2, tiles)),
            dma((4,)),
            dma((2,)),
            dma,
            dma,
            dma((pieces,)),
            dma((pieces,)),
        ]
    return pl.pallas_call(
        functools.partial(program, fused, tiles, bins, token_count),
        out_shape=jax.ShapeDtypeStruct((SCN, ROWS_DEV, GRID_W, channels), bf16),
        in_specs=specs,
        out_specs=pl.BlockSpec(memory_space=pltpu.VMEM),
        scratch_shapes=scratch,
        compiler_params=pltpu.CompilerParams(
            collective_id=0, has_side_effects=True, vmem_limit_bytes=60 * 1024 * 1024
        ),
    )(*operands)


def head_input_of(tokens, ln_gain, gate_weight, up_weight, down_weight, head_gain):
    inputs = tokens.astype(jnp.float32)
    normed = layer_norm(inputs, ln_gain).astype(jnp.bfloat16)
    axes = ("cam", "tile")
    gate_whole = lax.all_gather(gate_weight, axes, axis=0, tiled=True)
    up_whole = lax.all_gather(up_weight, axes, axis=0, tiled=True)
    gate = jnp.dot(normed, gate_whole, preferred_element_type=jnp.float32)
    up = jnp.dot(normed, up_whole, preferred_element_type=jnp.float32)
    hidden = (jax.nn.silu(gate) * up).astype(jnp.bfloat16)
    down_whole = lax.all_gather(down_weight.T, axes, axis=0, tiled=True)
    contract = (((1,), (1,)), ((), ()))
    branch = lax.dot_general(hidden, down_whole, contract, preferred_element_type=jnp.float32)
    return layer_norm(inputs + branch, head_gain).astype(jnp.bfloat16)


def on_device(
    tokens,
    ln_gain,
    gate_weight,
    up_weight,
    down_weight,
    head_gain,
    depth_weight,
    context_weight,
    slot_point,
    slot_cell,
    slot_count,
    conv1_weight,
    conv1_bias,
    conv2_weight,
    conv2_bias,
):
    tiles, cams = lax.axis_size("tile"), lax.axis_size("cam")
    token_count, width = tokens.shape
    bins, channels = depth_weight.shape[1], context_weight.shape[1]
    slots = [slot_point, slot_cell, slot_count]
    weights = [
        conv1_weight,
        conv1_bias.reshape(1, channels),
        conv2_weight,
        conv2_bias.reshape(1, channels),
    ]
    sizes = (tiles, bins, channels, token_count)
    rows, units = gate_weight.shape
    fused = cams == 4 and tiles % 4 == 0 and rows % 16 == 0 and (rows * tiles) % LANES == 0
    if not fused:
        head_input = head_input_of(
            tokens, ln_gain, gate_weight, up_weight, down_weight, head_gain
        )
        logits = lax.dot_general(
            depth_weight,
            head_input,
            (((0,), (1,)), ((), ())),
            preferred_element_type=jnp.float32,
        )
        context = jnp.dot(head_input, context_weight, preferred_element_type=jnp.float32)
        table = table_of(soft_depth(logits), context)
        return run(False, [table], slots, weights, sizes)
    arrays = [
        tokens,
        ln_gain.reshape(1, width),
        gate_weight,
        up_weight,
        down_weight.T,
        head_gain.reshape(1, width),
        depth_weight.T,
        context_weight,
    ]
    return run(True, arrays, slots, weights, sizes)


def solution(mesh):
    return jax.shard_map(
        on_device,
        mesh=mesh,
        in_specs=(
            P(("cam", "tile"), None),
            P(),
            P(("cam", "tile"), None),
            P(("cam", "tile"), None),
            P(None, ("cam", "tile")),
            P(),
            P(),
            P(),
            P(("cam", "tile"), None, None),
            P(("cam", "tile"), None, None),
            P(("cam", "tile"), None),
            P(),
            P(),
            P(),
            P(),
        ),
        out_specs=P("cam", "tile", None, None),
        check_vma=False,
    )
```

```python
import functools

import jax
import jax.numpy as jnp
from jax import lax
from jax.experimental import pallas as pl
from jax.experimental.pallas import tpu as pltpu
from jax.sharding import PartitionSpec as P

ROWS_DEV = 4
GRID_W = 256
SCN = 2
LANES = 128
MESH = pl.DeviceIdType.MESH


def layer_norm(values, gain):
    center = values - jnp.mean(values, axis=-1, keepdims=True)
    spread = jnp.mean(center * center, axis=-1, keepdims=True)
    return center * lax.rsqrt(spread + 1e-06) * gain


def remote(src, dst, send, recv, cam, tile):
    return pltpu.make_async_remote_copy(
        src_ref=src,
        dst_ref=dst,
        send_sem=send,
        recv_sem=recv,
        device_id={"cam": cam, "tile": tile},
        device_id_type=MESH,
    )


def soft_depth(logits):
    raised = jnp.exp(logits - jnp.max(logits, axis=0, keepdims=True))
    return raised / jnp.sum(raised, axis=0, keepdims=True)


def table_of(depth, context):
    bins, tokens = depth.shape
    rows = [context.astype(jnp.bfloat16)]
    depth = depth.astype(jnp.bfloat16)
    for first in range(0, tokens, LANES):
        block = depth[:, first : first + LANES]
        if block.shape[1] < LANES:
            blank = jnp.zeros((bins, LANES - block.shape[1]), jnp.bfloat16)
            block = jnp.concatenate([block, blank], axis=1)
        rows.append(block)
    return jnp.concatenate(rows, axis=0)


class Exchange:
    SPAN = ((0, 1), (1, 1), (2, 1), (0, 2))

    def __init__(self, tiles, own, whole, recv, sends):
        self.cam, self.tile = lax.axis_index("cam"), lax.axis_index("tile")
        self.tiles, self.depth = tiles, tiles // 2
        self.y, self.c = self.cam // 2, lax.rem(self.cam, 2)
        self.z, self.x = self.tile // 2, lax.rem(self.tile, 2)
        self.own, self.whole, self.recv = own, whole, recv
        self.up, self.down, self.side, self.core, self.pair = sends
        self.rows = own.shape[2]

    def shard(self, y, c, z, x):
        return (2 * y + c) * self.tiles + 2 * z + x

    def block(self, kind, shard):
        first, count = self.SPAN[kind]
        rows = pl.ds(pl.multiple_of(shard * self.rows, self.rows), self.rows)
        return self.whole.at[pl.ds(first, count), rows, :]

    def mine(self, kind, half):
        first, count = self.SPAN[kind]
        return self.own.at[half, pl.ds(first, count)]

    def to(self, route, kind, y, z, x):
        shard = self.shard(y, self.c, z, x)
        block = self.block(kind, shard)
        at = (kind, y, 2 * z + x)
        got = self.recv.at[kind, shard]
        if route == "up":
            return remote(block, block, self.up.at[at], got, self.cam, self.tile + 2)
        if route == "down":
            return remote(block, block, self.down.at[at], got, self.cam, self.tile - 2)
        if route == "side":
            other = 2 * (1 - self.y) + self.c
            return remote(block, block, self.side.at[at], got, other, self.tile)
        other = 2 * self.y + 1 - self.c
        return remote(block, block, self.core.at[at], got, other, self.tile)

    def across(self, kind):
        shard = self.shard(self.y, self.c, self.z, self.x)
        return remote(
            self.mine(kind, 1 - self.x),
            self.block(kind, shard),
            self.pair.at[kind],
            self.recv.at[kind, shard],
            self.cam,
            self.tile + 1 - 2 * self.x,
        )

    def wait(self, kind, y, c, z, x):
        shard = self.shard(y, c, z, x)
        block = self.block(kind, shard)
        remote(
            block, block, self.pair.at[kind], self.recv.at[kind, shard], self.cam, self.tile
        ).wait_recv()

    def spread(self, kind, y, x, side):
        def go_up():
            self.to("up", kind, y, self.z, x).start()

        def go_down():
            self.to("down", kind, y, self.z, x).start()

        if side:
            self.to("side", kind, y, self.z, x).start()
        pl.when(self.z + 1 < self.depth)(go_up)
        pl.when(self.z > 0)(go_down)
        self.to("core", kind, y, self.z, x).start()

    def units(self, late):
        mate = 1 - self.x
        if late:
            return ((2, self.y, self.x, True), (2, self.y, mate, True))
        return (
            (0, self.y, self.x, True),
            (1, self.y, self.x, False),
            (1, 1 - self.y, self.x, False),
            (3, self.y, mate, True),
        )

    def relay(self, late, d):
        def take(kind, y, z, x, side, more, route):
            self.wait(kind, y, self.c, z, x)
            if d + 1 < self.depth:
                pl.when(more)(lambda: self.to(route, kind, y, z, x).start())
            if side:
                self.to("side", kind, y, z, x).start()
            self.to("core", kind, y, z, x).start()

        for kind, y, x, side in self.units(late):

            def below():
                take(kind, y, self.z - d, x, side, self.z + 1 < self.depth, "up")

            def above():
                take(kind, y, self.z + d, x, side, self.z > 0, "down")

            pl.when(self.z - d >= 0)(below)
            pl.when(self.z + d < self.depth)(above)

    def crossed(self, late, z):
        for kind, y, x, side in self.units(late):
            if side:
                self.wait(kind, 1 - self.y, self.c, z, x)
                self.to("core", kind, 1 - self.y, z, x).start()

    def crossed_at(self, late, d):
        pl.when(self.z - d >= 0)(lambda: self.crossed(late, self.z - d))
        pl.when(self.z + d < self.depth)(lambda: self.crossed(late, self.z + d))

    def beside(self, late, y, zs):
        for z in zs:
            if late:
                for x in range(2):
                    self.wait(2, y, 1 - self.c, z, x)
            else:
                self.wait(0, y, 1 - self.c, z, self.x)
                self.wait(1, y, 1 - self.c, z, self.x)
                self.wait(3, y, 1 - self.c, z, 1 - self.x)

    def finish(self):
        self.across(3).wait_send()
        self.across(2).wait_send()
        for z in range(self.depth):
            for kind, y, x, side in (*self.units(False), *self.units(True)):

                def up():
                    self.to("up", kind, y, z, x).wait_send()

                def down():
                    self.to("down", kind, y, z, x).wait_send()

                pl.when((self.z >= z) & (self.z + 1 < self.depth))(up)
                pl.when((self.z <= z) & (self.z > 0))(down)
                self.to("core", kind, y, z, x).wait_send()
                if side:
                    self.to("side", kind, y, z, x).wait_send()
                    self.to("core", kind, 1 - y, z, x).wait_send()
        self.to("side", 1, self.y, self.z, self.x).wait_send()


def feed_forward(ex, tokens, gain, guest, normed, gate, up, hidden, kept, sent, came, sems, midway):
    local, tok_send, tok_recv, part_send, part_recv = sems
    count = tokens.shape[0]
    mate = ex.tile + 1 - 2 * ex.x
    token_copy = remote(tokens, guest, tok_send, tok_recv, ex.cam, mate)
    me = ex.shard(ex.y, ex.c, ex.z, ex.x)
    copies = [
        pltpu.make_async_copy(ex.mine(kind, ex.x), ex.block(kind, me), local.at[kind - 2])
        for kind in (3, 2)
    ]
    ex.across(3).start()
    for copy in copies:
        copy.start()
    copies[0].wait()
    ex.to("side", 1, ex.y, ex.z, ex.x).start()
    ex.spread(0, ex.y, ex.x, True)
    ex.spread(1, ex.y, ex.x, False)
    ex.across(2).start()
    token_copy.start()
    ex.wait(1, 1 - ex.y, ex.c, ex.z, ex.x)
    ex.spread(1, 1 - ex.y, ex.x, False)
    ex.wait(3, ex.y, ex.c, ex.z, 1 - ex.x)
    ex.spread(3, ex.y, 1 - ex.x, True)
    ex.relay(False, 1)
    ex.crossed(False, ex.z)
    for d in range(2, ex.depth - 1):
        ex.relay(False, d)
        ex.crossed_at(False, d - 1)
    copies[1].wait()
    ex.spread(2, ex.y, ex.x, True)
    ex.wait(2, ex.y, ex.c, ex.z, 1 - ex.x)
    ex.spread(2, ex.y, 1 - ex.x, True)
    token_copy.wait_recv()
    normed[count:] = layer_norm(guest[...].astype(jnp.float32), gain[...]).astype(jnp.bfloat16)
    wide = ex.rows * ex.tiles
    pieces = wide // LANES
    per_piece = ex.depth // pieces

    def project(cam, first):
        rows = pl.ds(pl.multiple_of(cam * wide, wide), wide)
        for which, total in ((0, gate), (1, up)):
            got = jnp.dot(
                normed[:, rows], ex.whole[which, rows, :], preferred_element_type=jnp.float32
            )
            if first:
                total[...] = got
            else:
                total[...] += got

    def part(piece):
        return remote(
            sent.at[piece], came.at[piece], part_send.at[piece], part_recv.at[piece], ex.cam, mate
        )

    def columns(cam, near):
        piece = cam * pieces + near
        rows = pl.ds(pl.multiple_of(piece * LANES, LANES), LANES)
        got = lax.dot_general(
            hidden[...],
            ex.whole[2, rows, :],
            (((1,), (1,)), ((), ())),
            preferred_element_type=jnp.float32,
        )
        kept[piece] = got[:count]
        sent[piece] = got[count:].astype(jnp.bfloat16)
        part(piece).start()

    every = range(ex.depth)
    ex.relay(False, ex.depth - 1)
    midway()
    project(2 * ex.y + ex.c, True)
    ex.crossed_at(False, ex.depth - 2)
    ex.relay(True, 1)
    ex.beside(False, ex.y, every)
    project(2 * ex.y + 1 - ex.c, False)
    ex.crossed_at(False, ex.depth - 1)
    project(2 * (1 - ex.y) + ex.c, False)
    for d in range(2, ex.depth - 1):
        ex.relay(True, d)
    ex.beside(False, 1 - ex.y, every)
    project(2 * (1 - ex.y) + 1 - ex.c, False)
    value = gate[...]
    hidden[...] = (value / (1.0 + jnp.exp(-value)) * up[...]).astype(jnp.bfloat16)
    for turn in range(pieces):
        near = lax.rem(ex.z // per_piece + turn, pieces)
        zs = [near * per_piece + i for i in range(per_piece)]
        if turn == pieces - 1:
            ex.relay(True, ex.depth - 1)
        columns(2 * ex.y + ex.c, near)
        ex.beside(True, ex.y, zs)
        columns(2 * ex.y + 1 - ex.c, near)
        for z in zs:
            ex.crossed(True, z)
        columns(2 * (1 - ex.y) + ex.c, near)
        ex.beside(True, 1 - ex.y, zs)
        columns(2 * (1 - ex.y) + 1 - ex.c, near)
    for piece in range(kept.shape[0]):
        part(piece).wait_recv()
    blocks = [kept[piece] + came[piece].astype(jnp.float32) for piece in range(kept.shape[0])]
    updated = tokens[...].astype(jnp.float32) + jnp.concatenate(blocks, axis=1)

    def finish():
        token_copy.wait_send()
        for piece in range(kept.shape[0]):
            part(piece).wait_send()
        ex.finish()

    return updated, finish


def one_hot(count, index):
    ids = lax.broadcasted_iota(jnp.int16, (count, index.shape[1]), 0)
    one, zero = jnp.array(1, jnp.bfloat16), jnp.array(0, jnp.bfloat16)
    return jnp.where(ids == index.astype(jnp.int16), one, zero)


def lift(table, packed, tokens, bins):
    point = packed // 65536
    token, depth_bin = point // bins, point % bins
    pick = one_hot(tokens, token)
    blocks = []
    for first in range(0, tokens, LANES):
        row = tokens + first // LANES * bins
        blocks.append(table[row : row + bins, : min(LANES, tokens - first)])
    depth = jnp.concatenate(blocks, axis=1)
    found = jnp.dot(depth, pick, preferred_element_type=jnp.float32)
    bin_ids = lax.broadcasted_iota(jnp.int32, found.shape, 0)
    weight = jnp.sum(jnp.where(bin_ids == depth_bin, found, 0.0), axis=0, keepdims=True)
    context = lax.dot_general(
        table[:tokens], pick, (((0,), (0,)), ((), ())), preferred_element_type=jnp.float32
    )
    return weight * context


def add_scene(total, scene, lifted, packed):
    half = total.shape[1]
    cell = packed % 65536
    part = cell // half
    low = jnp.where(part == 2 * scene, lifted, 0.0)
    high = jnp.where(part == 2 * scene + 1, lifted, 0.0)
    both = jnp.concatenate([low, high], axis=0).astype(jnp.bfloat16)
    place = one_hot(half, cell % half)
    total[scene] += lax.dot_general(
        place, both, (((1,), (1,)), ((), ())), preferred_element_type=jnp.float32
    )


class Tables:
    def __init__(self, tiles, held, sends, recv):
        self.cam, self.tile = lax.axis_index("cam"), lax.axis_index("tile")
        self.depth = tiles // 2
        self.z, self.x = self.tile // 2, lax.rem(self.tile, 2)
        self.held, self.recv = held, recv
        self.up, self.down, self.pair = sends

    def to(self, route, z):
        source = 2 * z + self.x
        dst = self.held.at[source]
        src = dst
        got = self.recv.at[source]
        if route == "up":
            return remote(src, dst, self.up.at[z], got, self.cam, self.tile + 2)
        if route == "down":
            return remote(src, dst, self.down.at[z], got, self.cam, self.tile - 2)
        return remote(src, dst, self.pair.at[z], got, self.cam, self.tile + 1 - 2 * self.x)

    def wait(self, source):
        dst = self.held.at[source]
        remote(dst, dst, self.pair.at[0], self.recv.at[source], self.cam, self.tile).wait_recv()

    def begin(self):
        pl.when(self.z + 1 < self.depth)(lambda: self.to("up", self.z).start())
        pl.when(self.z > 0)(lambda: self.to("down", self.z).start())
        self.to("pair", self.z).start()

    def relay(self, d):
        def take(z, more, route):
            self.wait(2 * z + self.x)
            pl.when(more)(lambda: self.to(route, z).start())
            self.to("pair", z).start()

        up, down = self.z + 1 < self.depth, self.z > 0
        pl.when(self.z - d >= 0)(lambda: take(self.z - d, up, "up"))
        pl.when(self.z + d < self.depth)(lambda: take(self.z + d, down, "down"))

    def source(self, turn):
        step = turn // 2
        if self.depth & (self.depth - 1) == 0:
            z = self.z ^ step
        else:
            z = lax.rem(self.z + step, self.depth)
        return 2 * z + (self.x ^ lax.rem(turn, 2))

    def between(self, turn):
        pl.when((turn > 0) & (turn < self.depth))(lambda: self.relay(turn))
        pl.when(lax.rem(turn, 2) == 1)(lambda: self.wait(self.source(turn)))

    def finish(self):
        for z in range(self.depth):
            up = (self.z >= z) & (self.z + 1 < self.depth)
            pl.when(up)(lambda: self.to("up", z).wait_send())
            pl.when((self.z <= z) & (self.z > 0))(lambda: self.to("down", z).wait_send())
            self.to("pair", z).wait_send()


def fill_slots(point, cell, count, slots, points):
    tiles, _, width = slots.shape
    used = point.shape[2]
    ids = lax.broadcasted_iota(jnp.int32, (1, used), 1)
    for k in range(tiles):
        if used < width:
            slots[k] = jnp.full((1, width), points * 65536, jnp.int32)
        live = ids < count[0, k]
        row = jnp.where(live, point[0, k : k + 1, :], points) * 65536
        slots[k, :, :used] = row + cell[0, k : k + 1, :]


def fill_own(gate, up, down, own):
    units = gate.shape[1]
    width = own.shape[3]
    even = units - units % LANES
    for half in range(2):
        first = half * width
        full = min(width, even - first)
        for which, ref in ((0, gate), (1, up), (2, down)):
            own[half, which, :, :full] = ref[:, first : first + full]
            if full < width:
                rest = units - first - full
                blank = jnp.zeros((own.shape[2], width - full), jnp.bfloat16)
                own[half, which, :, full:] = blank
                if rest > 0:
                    tail = ref[:, first + full : units]
                    own[half, which, :, full : full + rest] = tail


def widen(source, index, wide, row):
    value = source[index].astype(jnp.float32)
    columns, channels = value.shape
    places = lax.broadcasted_iota(jnp.int32, (columns, channels), 0)
    left = jnp.where(places == 0, 0.0, pltpu.roll(value, 1, 0))
    right = jnp.where(places == columns - 1, 0.0, pltpu.roll(value, columns - 1, 0))
    wide[row] = jnp.concatenate([left, value, right], axis=1).astype(jnp.bfloat16)


def convolve(wide, row, weight):
    total = None
    for shift in range(3):
        taps = weight[shift].reshape(wide.shape[2], -1)
        got = jnp.dot(wide[row + shift], taps, preferred_element_type=jnp.float32)
        total = got if total is None else total + got
    return total


def program(fused, tiles, bins, token_count, *refs):
    count = 14 if fused else 7
    operands, out, fetched, fetch = refs[:count], refs[count + 1], refs[-count:], refs[-count - 1]
    live = refs[count]
    refs = refs[count + 2 : -count - 1]
    fetches = [
        pltpu.make_async_copy(operand, place, fetch.at[i])
        for i, (operand, place) in enumerate(zip(operands, fetched))
    ]
    (point, cell, w1, b1, w2, b2) = fetched[-6:]
    if fused:
        (tokens, gain, w_gate, w_up, w_down, head_gain, w_depth, w_context) = fetched[:8]
    else:
        table_in = fetched[0]
    (slot_in, slots, held, lifted, total, ext, wide, mid, wide_mid) = refs[:9]
    (slot_send, slot_recv, t_up, t_down, t_pair, t_recv, halo_send, halo_recv) = refs[9:17]
    if fused:
        (own, whole, guest, normed, gate, up, hidden, kept, sent, came) = refs[17:27]
        (recv, zup, zdown, side, core, pair) = refs[27:33]
        sems = refs[33:38]
    cam, me = lax.axis_index("cam"), lax.axis_index("tile")
    barrier = pltpu.get_barrier_semaphore()

    def hello(other_cam, other_tile):
        pl.semaphore_signal(
            barrier, inc=1, device_id={"cam": other_cam, "tile": other_tile}, device_id_type=MESH
        )

    soon = (0, 1, 2, 3, 4, 8, 9) if fused else range(count)
    for i in (*soon, *(i for i in range(count) if i not in soon)):
        fetches[i].start()
    if fused:
        y, c = cam // 2, lax.rem(cam, 2)
        before, after = me >= 2, me + 2 < tiles
        hello(2 * y + 1 - c, me)
        hello(2 * (1 - y) + c, me)
        hello(cam, me + 1 - 2 * lax.rem(me, 2))
        pl.when(before)(lambda: hello(cam, me - 2))
        pl.when(after)(lambda: hello(cam, me + 2))
        expected = 3 + jnp.where(before, 1, 0) + jnp.where(after, 1, 0)
        for i in soon:
            fetches[i].wait()
        fill_own(w_gate, w_up, w_down, own)
        normed[:token_count] = layer_norm(tokens[...].astype(jnp.float32), gain[...]).astype(
            jnp.bfloat16
        )
    else:

        def greet(k, carry):
            hello(cam, lax.rem(me + k, tiles))
            return carry

        lax.fori_loop(1, tiles, greet, 0)
        expected = tiles - 1
        for i in soon:
            fetches[i].wait()
    fill_slots(point, cell, live, slot_in, token_count * bins)
    pl.semaphore_wait(barrier, expected)

    def slot_copy(k):
        other = lax.rem(me + k, tiles)
        return remote(slot_in.at[other], slots.at[me], slot_send.at[k], slot_recv.at[k], cam, other)

    def slot_wait(k):
        source = lax.rem(me - k + tiles, tiles)
        remote(
            slot_in.at[me], slots.at[source], slot_send.at[k], slot_recv.at[k], cam, me
        ).wait_recv()

    def slot_start(k, carry):
        slot_copy(k).start()
        return carry

    def slot_finish(k, carry):
        slot_wait(k)
        slot_copy(k).wait_send()
        return carry

    own_slots = pltpu.make_async_copy(slot_in.at[me], slots.at[me], slot_send.at[0])

    def send_slots():
        lax.fori_loop(1, tiles, slot_start, 0)
        own_slots.start()

    if fused:
        ex = Exchange(tiles, own, whole, recv, (zup, zdown, side, core, pair))
        updated, finish = feed_forward(
            ex, tokens, gain, guest, normed, gate, up, hidden, kept, sent, came, sems, send_slots
        )
        for i in range(count):
            if i not in soon:
                fetches[i].wait()
        head_input = layer_norm(updated, head_gain[...]).astype(jnp.bfloat16)
        logits = lax.dot_general(
            w_depth[...], head_input, (((1,), (1,)), ((), ())), preferred_element_type=jnp.float32
        )
        context = jnp.dot(head_input, w_context[...], preferred_element_type=jnp.float32)
        held[me] = table_of(soft_depth(logits), context)
    else:
        send_slots()
        held[me] = table_in[...]
    tables = Tables(tiles, held, (t_up, t_down, t_pair), t_recv)
    tables.begin()
    own_slots.wait()
    lax.fori_loop(1, tiles, slot_finish, 0)
    total[...] = jnp.zeros_like(total)
    channels = ext.shape[3]
    rows_ext, rows_mid = ROWS_DEV + 4, ROWS_DEV + 2
    has_before, has_after = me > 0, me + 1 < tiles
    blank = jnp.zeros((SCN, 2, GRID_W, channels), jnp.bfloat16)

    def first_tile():
        ext[:, 0:2] = blank

    def last_tile():
        ext[:, ROWS_DEV + 2 : ROWS_DEV + 4] = blank

    pl.when(me == 0)(first_tile)
    pl.when(me + 1 == tiles)(last_tile)

    def halo(which, scene):
        if which == 0:
            src, dst, other = ext.at[scene, 2:4], ext.at[scene, ROWS_DEV + 2 : ROWS_DEV + 4], me - 1
        else:
            src, dst, other = ext.at[scene, ROWS_DEV : ROWS_DEV + 2], ext.at[scene, 0:2], me + 1
        at = (which, scene)
        return remote(src, dst, halo_send.at[at], halo_recv.at[at], cam, other)

    early = 3 * tiles // 8

    def first_pass(turn, carry):
        tables.between(turn)
        source = tables.source(turn)
        packed = slots[source]
        value = lift(held.at[source], packed, token_count, bins)
        lifted[source] = value.astype(jnp.bfloat16)
        add_scene(total, 0, value, packed)

        def more_scenes():
            for scene in range(1, SCN):
                add_scene(total, scene, value, packed)

        pl.when(turn < early)(more_scenes)
        return carry

    lax.fori_loop(0, tiles, first_pass, 0)
    for scene in range(SCN):
        if scene > 0:

            def next_pass(turn, carry):
                source = tables.source(turn)
                add_scene(total, scene, lifted[source].astype(jnp.float32), slots[source])
                return carry

            lax.fori_loop(early, tiles, next_pass, 0)
        for row in range(ROWS_DEV):
            side_of, first = divmod(row * GRID_W, total.shape[1])
            ext[scene, 2 + row] = total[
                scene, first : first + GRID_W, side_of * channels : (side_of + 1) * channels
            ].astype(jnp.bfloat16)
        pl.when(has_before)(lambda: halo(0, scene).start())
        pl.when(has_after)(lambda: halo(1, scene).start())
    for scene in range(SCN):
        for row in range(2, ROWS_DEV + 2):
            widen(ext, (scene, row), wide, scene * rows_ext + row)
    for scene in range(SCN):
        pl.when(has_before)(lambda: halo(1, scene).wait_recv())
        pl.when(has_after)(lambda: halo(0, scene).wait_recv())
        for row in (0, 1, ROWS_DEV + 2, ROWS_DEV + 3):
            widen(ext, (scene, row), wide, scene * rows_ext + row)
        for row in range(rows_mid):
            value = jnp.maximum(convolve(wide, scene * rows_ext + row, w1) + b1[...], 0.0)
            if row == 0:
                value = jnp.where(has_before, value, 0.0)
            if row == rows_mid - 1:
                value = jnp.where(has_after, value, 0.0)
            mid[scene, row] = value.astype(jnp.bfloat16)
            widen(mid, (scene, row), wide_mid, scene * rows_mid + row)
        for row in range(ROWS_DEV):
            value = convolve(wide_mid, scene * rows_mid + row, w2) + b2[...]
            value = ext[scene, 2 + row].astype(jnp.float32) + value
            out[scene, row] = value.astype(jnp.bfloat16)
    for scene in range(SCN):
        pl.when(has_before)(lambda: halo(0, scene).wait_send())
        pl.when(has_after)(lambda: halo(1, scene).wait_send())
    tables.finish()
    if fused:
        finish()


def run(fused, arrays, slots, weights, sizes):
    tiles, bins, channels, token_count = sizes
    cells = SCN * ROWS_DEV * GRID_W
    dma = pltpu.SemaphoreType.DMA
    bf16, f32 = jnp.bfloat16, jnp.float32
    slot_count = slots[0].shape[2]
    slot_width = slot_count + -slot_count % LANES
    table_rows = token_count + bins * pl.cdiv(token_count, LANES)
    scratch = [
        pltpu.VMEM((tiles, 1, slot_width), jnp.int32),
        pltpu.VMEM((tiles, 1, slot_width), jnp.int32),
        pltpu.VMEM((tiles, table_rows, LANES), bf16),
        pltpu.VMEM((tiles, channels, slot_width), bf16),
        pltpu.VMEM((SCN, cells // SCN // 2, 2 * channels), f32),
        pltpu.VMEM((SCN, ROWS_DEV + 4, GRID_W, channels), bf16),
        pltpu.VMEM((SCN * (ROWS_DEV + 4), GRID_W, 3 * channels), bf16),
        pltpu.VMEM((SCN, ROWS_DEV + 2, GRID_W, channels), bf16),
        pltpu.VMEM((SCN * (ROWS_DEV + 2), GRID_W, 3 * channels), bf16),
        dma((tiles,)),
        dma((tiles,)),
        dma((tiles // 2,)),
        dma((tiles // 2,)),
        dma((tiles // 2,)),
        dma((tiles,)),
        dma((2, SCN)),
        dma((2, SCN)),
    ]
    operands = [*arrays, *slots[:2], *weights]
    specs = [pl.BlockSpec(memory_space=pl.ANY)] * len(operands)
    specs += [pl.BlockSpec(memory_space=pltpu.SMEM)]
    if fused:
        tokens, gate_weight = arrays[0], arrays[2]
        count, width = tokens.shape
        rows, units = gate_weight.shape
        cams = lax.axis_size("cam")
        half = (units + -units % (2 * LANES)) // 2
        pieces = width // LANES
        scratch += [
            pltpu.VMEM((2, 3, rows, half), bf16),
            pltpu.VMEM((3, width, half), bf16),
            pltpu.VMEM((count, width), bf16),
            pltpu.VMEM((2 * count, width), bf16),
            pltpu.VMEM((2 * count, half), f32),
            pltpu.VMEM((2 * count, half), f32),
            pltpu.VMEM((2 * count, half), bf16),
            pltpu.VMEM((pieces, count, LANES), f32),
            pltpu.VMEM((pieces, count, LANES), bf16),
            pltpu.VMEM((pieces, count, LANES), bf16),
            dma((4, cams * tiles)),
            dma((4, 2, tiles)),
            dma((4, 2, tiles)),
            dma((4, 2, tiles)),
            dma((4, 2, tiles)),
            dma((4,)),
            dma((2,)),
            dma,
            dma,
            dma((pieces,)),
            dma((pieces,)),
        ]
    scratch += [dma((len(operands),))]
    scratch += [pltpu.VMEM(operand.shape, operand.dtype) for operand in operands]
    return pl.pallas_call(
        functools.partial(program, fused, tiles, bins, token_count),
        out_shape=jax.ShapeDtypeStruct((SCN, ROWS_DEV, GRID_W, channels), bf16),
        in_specs=specs,
        out_specs=pl.BlockSpec(memory_space=pltpu.VMEM),
        scratch_shapes=scratch,
        compiler_params=pltpu.CompilerParams(
            collective_id=0, has_side_effects=True, vmem_limit_bytes=60 * 1024 * 1024
        ),
    )(*operands, slots[2])


def head_input_of(tokens, ln_gain, gate_weight, up_weight, down_weight, head_gain):
    inputs = tokens.astype(jnp.float32)
    normed = layer_norm(inputs, ln_gain).astype(jnp.bfloat16)
    axes = ("cam", "tile")
    gate_whole = lax.all_gather(gate_weight, axes, axis=0, tiled=True)
    up_whole = lax.all_gather(up_weight, axes, axis=0, tiled=True)
    gate = jnp.dot(normed, gate_whole, preferred_element_type=jnp.float32)
    up = jnp.dot(normed, up_whole, preferred_element_type=jnp.float32)
    hidden = (jax.nn.silu(gate) * up).astype(jnp.bfloat16)
    down_whole = lax.all_gather(down_weight.T, axes, axis=0, tiled=True)
    contract = (((1,), (1,)), ((), ()))
    branch = lax.dot_general(hidden, down_whole, contract, preferred_element_type=jnp.float32)
    return layer_norm(inputs + branch, head_gain).astype(jnp.bfloat16)


def on_device(
    tokens,
    ln_gain,
    gate_weight,
    up_weight,
    down_weight,
    head_gain,
    depth_weight,
    context_weight,
    slot_point,
    slot_cell,
    slot_count,
    conv1_weight,
    conv1_bias,
    conv2_weight,
    conv2_bias,
):
    tiles, cams = lax.axis_size("tile"), lax.axis_size("cam")
    token_count, width = tokens.shape
    bins, channels = depth_weight.shape[1], context_weight.shape[1]
    slots = [slot_point, slot_cell, slot_count]
    weights = [
        conv1_weight,
        conv1_bias.reshape(1, channels),
        conv2_weight,
        conv2_bias.reshape(1, channels),
    ]
    sizes = (tiles, bins, channels, token_count)
    rows, units = gate_weight.shape
    fused = cams == 4 and tiles % 4 == 0 and rows % 16 == 0 and (rows * tiles) % LANES == 0
    if not fused:
        head_input = head_input_of(
            tokens, ln_gain, gate_weight, up_weight, down_weight, head_gain
        )
        logits = lax.dot_general(
            depth_weight,
            head_input,
            (((0,), (1,)), ((), ())),
            preferred_element_type=jnp.float32,
        )
        context = jnp.dot(head_input, context_weight, preferred_element_type=jnp.float32)
        table = table_of(soft_depth(logits), context)
        return run(False, [table], slots, weights, sizes)
    arrays = [
        tokens,
        ln_gain.reshape(1, width),
        gate_weight,
        up_weight,
        down_weight.T,
        head_gain.reshape(1, width),
        depth_weight.T,
        context_weight,
    ]
    return run(True, arrays, slots, weights, sizes)


def solution(mesh):
    return jax.shard_map(
        on_device,
        mesh=mesh,
        in_specs=(
            P(("cam", "tile"), None),
            P(),
            P(("cam", "tile"), None),
            P(("cam", "tile"), None),
            P(None, ("cam", "tile")),
            P(),
            P(),
            P(),
            P(("cam", "tile"), None, None),
            P(("cam", "tile"), None, None),
            P(("cam", "tile"), None),
            P(),
            P(),
            P(),
            P(),
        ),
        out_specs=P("cam", "tile", None, None),
        check_vma=False,
    )
```
